32 devices in a mesh: pair: 8 (over y, x, core), grp: 4 (over z).
Axes of the slice: x: 2, y: 2, z: 4, core: 2. Of those that a mesh axis runs over, the one named last changes fastest.
Arguments:
- amplitudes: float32 [64, 64, 4096], P('pair'), may hold values from -6 to 6
- integrals: float32 [4, 8, 4, 64, 4096], P('grp', 'pair'), may hold values from -0.09375 to 0.09375
- tasks: int32 [4, 8, 4], P('grp', 'pair'), may hold values from -1 to 63, as said below
Outputs:
- residual: float32 [4, 512, 64], P('grp', 'pair')
The draws below stay inside these ranges and needn't reach their ends.
Inputs may be any that keep to these rules, and one draw needn't show every extreme that they name: `tasks`: in each device's list the live entries (not -1) come first and are distinct; every device has at least one live entry, and in every index of grp some device has all 4 live.
All inputs are finite; a program needn't handle non-finite values.
Results may differ from the reference program's by a relative error of at most 0.0003.
Values sent between devices are 32-bit elements; how exact they have to be, the bound alone decides.
A program may use at most 128 MiB of HBM per device.

```python
import jax
import jax.numpy as jnp
from jax import lax

TS = 64
NT = 8
SLOT_DEV = 4
NCD = 64
PAIRS = 64
N_PAIR = 8
N_GRP = 4


def draw_tasks(key, part):
    choice_count = NT * (NT * NT // N_PAIR)
    key_count, key_full, key_perm = jax.random.split(key, 3)
    counts = jax.random.randint(key_count, (N_GRP, N_PAIR), 1, SLOT_DEV + 1)
    full_device = jax.random.randint(key_full, (N_GRP,), 0, N_PAIR)
    counts = jnp.where(jnp.arange(N_PAIR)[None, :] == full_device[:, None], SLOT_DEV, counts)
    perm_keys = jax.random.split(key_perm, N_GRP * N_PAIR)
    picked = jax.vmap(lambda single: jax.random.permutation(single, choice_count)[:SLOT_DEV])(perm_keys)
    picked = picked.reshape(N_GRP, N_PAIR, SLOT_DEV)
    filled = jnp.arange(SLOT_DEV)[None, None, :] < counts[..., None]
    return jnp.where(filled, picked, -1).astype(jnp.int32)


def levels(own_key, dims, cuts, low, top_value):
    gain = 1.0
    for axis_at, blocks in cuts:
        heights = jax.random.uniform(jax.random.fold_in(jax.random.fold_in(own_key, 6), axis_at), (blocks,), jnp.float32, low / len(cuts), top_value / len(cuts))
        gain = gain * jnp.repeat(jnp.exp(heights), dims[axis_at] // blocks).reshape((-1,) + (1,) * (len(dims) - 1 - axis_at))
    return gain


def bell_draw(rng, shape, width, limit, cuts=(), kind=jnp.bfloat16):
    array = width * jax.random.normal(rng, shape, jnp.float32)
    if cuts:
        array = array * levels(rng, shape, cuts, -0.22, 0.18)
    return jnp.clip(array, -limit, limit).astype(kind)


def setup_inputs(seed: int = 0) -> dict:
    seeds = jax.random.split(jax.random.key(seed), 4)
    return {
        "amplitudes": bell_draw(seeds[0], (PAIRS, NCD, TS * TS), 1.0, 6.0, ((0, 8),), jnp.float32),
        "integrals": bell_draw(seeds[1], (N_GRP, N_PAIR, SLOT_DEV, TS, TS * TS), (TS * TS) ** -0.5, 0.09375, ((0, 4), (1, 8)), jnp.float32),
        "tasks": draw_tasks(jax.random.fold_in(seeds[3], 71), 0),
    }


def reference(amplitudes, integrals, tasks):
    local_pairs = NT * NT // N_PAIR

    def one_group(group_args):
        blocks, codes = group_args
        valid = codes >= 0
        safe = jnp.maximum(codes, 0)
        column = jnp.arange(N_PAIR, dtype=jnp.int32)[:, None] * local_pairs + safe % local_pairs
        chosen = amplitudes[:, column, :]
        contrib = jnp.einsum("qkrc,pqkc->qkrp", blocks, chosen, precision=lax.Precision.HIGHEST)
        onehot = ((safe // local_pairs)[..., None] == jnp.arange(NT, dtype=jnp.int32)) & valid[..., None]
        onehot = onehot.astype(jnp.float32)
        total = jnp.einsum("qkb,qkrp->brp", onehot, contrib, precision=lax.Precision.HIGHEST)
        return total.reshape(NT * TS, PAIRS)

    return lax.map(one_group, (integrals, tasks))
```

```python
import functools

import jax
import jax.numpy as jnp
from jax import lax
from jax.experimental import pallas as pl
from jax.experimental.pallas import tpu as pltpu
from jax.sharding import PartitionSpec as P

NT = 8
SHARED = 3840
CHUNKS = 5
MESH = pl.DeviceIdType.MESH


def split(x):
    high = x.astype(jnp.bfloat16)
    low = (x - high.astype(jnp.float32)).astype(jnp.bfloat16)
    return jnp.concatenate([high, low], axis=0)


def kernel(n, layers, columns, shared, pack, tasks_ref, amp_ref, int_ref, out_ref, listed, amp, blocks, rows, sent,
           held, chosen, both, total, parts, local_sem, list_send, list_recv, send_sem, recv_sem,
           tail_send, tail_recv, fetch_send, fetch_recv, layer_send, layer_recv, part_send, part_recv, *far):
    me = lax.axis_index("pair")
    grp = lax.axis_index("grp")
    own_rows, pairs, depth = amp_ref.shape
    slots, width, _ = int_ref.shape
    local = pairs // n
    per = local // layers if shared else 1
    part_rows = out_ref.shape[0]
    lists = columns < local
    chunk = shared // CHUNKS
    near = n - 3 if shared else n - 1

    load_amp = pltpu.make_async_copy(amp_ref, amp, local_sem.at[0])
    load_int = pltpu.make_async_copy(int_ref, blocks, local_sem.at[1])
    load_amp.start()
    load_int.start()

    def other(d):
        if shared:
            y = lax.rem(me // 4 + d // 4, 2)
            x = lax.rem(me // 2 + d // 2, 2)
            return y * 4 + x * 2 + lax.rem(me + d, 2)
        return lax.rem(me + d, n)

    def near_peer(i):
        if shared:
            return other(jnp.where(i < 4, 2 + 2 * lax.rem(i, 2) + i // 2, 1))
        return other(i + 1)

    def target(p):
        return (p, grp)

    barrier = pltpu.get_barrier_semaphore()

    @pl.loop(1, n)
    def _(d):
        pl.semaphore_signal(barrier, inc=1, device_id=target(other(d)), device_id_type=MESH)

    if shared:
        @pl.when(grp > 0)
        def _():
            pl.semaphore_signal(barrier, inc=1, device_id=(me, grp - 1), device_id_type=MESH)

        @pl.when(grp < layers - 1)
        def _():
            pl.semaphore_signal(barrier, inc=1, device_id=(me, grp + 1), device_id_type=MESH)

        for f in range(2):
            p = other(6 + f)
            for c in range(columns):
                held[c, p] = jnp.zeros_like(held[c, p])
        chosen[...] = jnp.zeros_like(chosen)

        peers = n - 1 + jnp.minimum(grp, 1) + jnp.minimum(layers - 1 - grp, 1)
        pl.semaphore_wait(barrier, peers)
    else:
        pl.semaphore_wait(barrier, n - 1)

    def list_copy(frm, to):
        return pltpu.make_async_remote_copy(
            src_ref=tasks_ref, dst_ref=listed.at[frm], send_sem=list_send.at[to], recv_sem=list_recv.at[frm],
            device_id=target(to), device_id_type=MESH)

    def column_copy(c, frm, to):
        return pltpu.make_async_remote_copy(
            src_ref=sent.at[c, to], dst_ref=held.at[c, frm], send_sem=send_sem.at[c, to],
            recv_sem=recv_sem.at[c, frm], device_id=target(to), device_id_type=MESH)

    def tail_copy(c, f, frm, to):
        tail = pl.ds(shared, depth - shared)
        return pltpu.make_async_remote_copy(
            src_ref=sent.at[c, to, :, tail], dst_ref=held.at[c, frm, :, tail], send_sem=tail_send.at[c, f],
            recv_sem=tail_recv.at[c, f], device_id=target(to), device_id_type=MESH)

    def fetch_copy(q, j, f):
        to = other(6 + f)
        return pltpu.make_async_remote_copy(
            src_ref=amp_ref.at[:, to * local + grp * per + j, pl.ds(q * chunk, chunk)],
            dst_ref=far[q].at[grp * per + j, f],
            send_sem=fetch_send.at[q, j, f], recv_sem=fetch_recv.at[q, j, f], device_id=target(to),
            device_id_type=MESH)

    def layer_copy(block, q, j, step):
        at = far[q].at[block * per + j]
        return pltpu.make_async_remote_copy(
            src_ref=at, dst_ref=at, send_sem=layer_send.at[(step + 1) // 2, q, block * per + j],
            recv_sem=layer_recv.at[q, block * per + j], device_id=(me, grp + step), device_id_type=MESH)

    def part_copy(frm, to):
        return pltpu.make_async_remote_copy(
            src_ref=total.at[to], dst_ref=parts.at[frm], send_sem=part_send.at[to],
            recv_sem=part_recv.at[frm], device_id=target(to), device_id_type=MESH)

    if lists:
        @pl.loop(1, n)
        def _(d):
            list_copy(me, other(d)).start()

    units = [(q, j) for q in range(CHUNKS) for j in range(per)] if shared else []
    for q, j in units:
        for f in range(2):
            fetch_copy(q, j, f).start()

    load_amp.wait()

    if lists:
        @pl.loop(1, n)
        def _(d):
            list_copy(other(d), other(d)).wait_recv()

    def column(p, c, codes):
        if lists:
            return p * local + lax.rem(jnp.maximum(codes(c), 0), local)
        return p * local + c

    def send(c):
        @pl.loop(0, near)
        def _(i):
            p = near_peer(i)
            at = column(p, c, lambda k: listed[p, 0, k])
            for row in range(own_rows):
                sent[c, p, pl.ds(row, 1), :] = amp[row, pl.ds(at, 1), :]
            column_copy(c, me, p).start()

        if shared and shared < depth:
            for f in range(2):
                p = other(6 + f)
                at = column(p, c, lambda k: listed[p, 0, k])
                for row in range(own_rows):
                    sent[c, p, pl.ds(row, 1), pl.ds(shared, depth - shared)] = amp[
                        row, pl.ds(at, 1), pl.ds(shared, depth - shared)]
                tail_copy(c, f, me, p).start()

        at = column(me, c, lambda k: tasks_ref[0, k])
        for row in range(own_rows):
            held[c, me, pl.ds(row, 1), :] = amp[row, pl.ds(at, 1), :]

    def forward(hop, q, j, act):
        @pl.when((grp - hop >= 0) & (grp + 1 < layers))
        def _():
            act(layer_copy(grp - hop, q, j, 1))

        @pl.when((grp + hop < layers) & (grp >= 1))
        def _():
            act(layer_copy(grp + hop, q, j, -1))

    def stage(hop, chosen_units):
        for q, j in chosen_units:
            if hop == 0:
                for f in range(2):
                    fetch_copy(q, j, f).wait_recv()
            else:
                @pl.when(grp - hop >= 0)
                def _():
                    layer_copy(grp - hop, q, j, 1).wait_recv()

                @pl.when(grp + hop < layers)
                def _():
                    layer_copy(grp + hop, q, j, -1).wait_recv()

            if hop < layers - 1:
                forward(hop, q, j, lambda copy: copy.start())

    def arrive(c):
        @pl.loop(0, near)
        def _(i):
            p = near_peer(i)
            column_copy(c, p, p).wait_recv()

        if shared and shared < depth:
            for f in range(2):
                p = other(6 + f)
                tail_copy(c, f, p, p).wait_recv()

    def multiply(slot, operand, span):
        operand = operand.reshape(n * own_rows, operand.shape[-1])
        return lax.dot_general(rows[slot, :, span], split(operand), (((1,), (1,)), ((), ())),
                               preferred_element_type=jnp.float32)

    def picked(slot):
        return lax.rem(jnp.maximum(tasks_ref[0, slot], 0), local)

    def far_part(q):
        for slot in range(slots):
            for f in range(2):
                chosen[slot, other(6 + f)] = far[q][picked(slot), f]
            both[slot] += multiply(slot, chosen[slot], pl.ds(q * chunk, chunk))

    whole = pl.ds(0, depth)

    def convert():
        @pl.loop(0, slots)
        def _(slot):
            rows[slot] = split(blocks[slot])

    if shared:
        edges = [len(units) * i // columns for i in range(columns + 1)]
        for c in range(columns):
            send(c)
            stage(0, units[edges[c]: edges[c + 1]])
        load_int.wait()
        convert()
        stage(1, units)
        arrive(0)
        both[0] = multiply(0, held[0], whole)
        stage(2, units[:len(units) // 2])
        arrive(1)
        both[1] = multiply(1, held[1], whole)
        stage(2, units[len(units) // 2:])
        arrive(2)
        both[2] = multiply(2, held[2], whole)
        for q in range(CHUNKS - 1):
            stage(3, [(q, j) for j in range(per)])
            far_first = q == 0
            if far_first:
                both[3] = jnp.zeros_like(both[3])
            far_part(q)
        arrive(3)
        both[3] += multiply(3, held[3], whole)
        stage(3, [(CHUNKS - 1, j) for j in range(per)])
        far_part(CHUNKS - 1)
    else:
        for c in range(columns):
            send(c)
        load_int.wait()
        convert()
        for c in range(columns):
            arrive(c)

        @pl.loop(0, slots)
        def _(slot):
            both[slot] = multiply(slot, held[picked(slot)], whole)

    held_rows = n * own_rows
    piece = part_rows // pack
    tiles = []
    terms = []
    for slot in range(slots):
        code = tasks_ref[0, slot]
        tiles.append(jnp.where(code >= 0, lax.div(jnp.maximum(code, 0), local), -1))
        whole_term = both[slot]
        whole_term = whole_term[:width] + whole_term[width:]
        terms.append(whole_term[:, :held_rows] + whole_term[:, held_rows:])
    packed = {}
    for p in range(n):
        first = p * part_rows
        low = first % width
        value = jnp.zeros(total.shape[1:], jnp.float32)
        for slot in range(slots):
            if (slot, low) not in packed:
                packed[slot, low] = jnp.concatenate(
                    [terms[slot][low + i * piece: low + (i + 1) * piece] for i in range(pack)], axis=1)
            value += jnp.where(tiles[slot] == first // width, packed[slot, low], 0.0)
        total[p] = value

    @pl.loop(1, n)
    def _(d):
        part_copy(me, other(d)).start()

    parts[me] = total[me]

    @pl.loop(1, n)
    def _(d):
        part_copy(other(d), other(d)).wait_recv()

    result = parts[0]
    for p in range(1, n):
        result += parts[p]
    for i in range(pack):
        out_ref[i * piece: (i + 1) * piece, :] = result[:, i * held_rows: (i + 1) * held_rows]

    if shared:
        for q, j in units:
            for f in range(2):
                fetch_copy(q, j, f).wait_send()
            for hop in range(layers - 1):
                forward(hop, q, j, lambda copy: copy.wait_send())
        if shared < depth:
            for c in range(columns):
                for f in range(2):
                    tail_copy(c, f, me, other(6 + f)).wait_send()

    @pl.loop(1, n)
    def _(d):
        part_copy(me, other(d)).wait_send()
        if lists:
            list_copy(me, other(d)).wait_send()

    @pl.loop(0, near)
    def _(i):
        for c in range(columns):
            column_copy(c, me, near_peer(i)).wait_send()


def body(n, layers, amplitudes, integrals, tasks):
    own_rows, pairs, depth = amplitudes.shape
    slots, width = integrals.shape[2:4]
    local = pairs // n
    columns = min(local, slots)
    part_rows = NT * width // n
    held_rows = n * own_rows
    pack = max(1, 128 // held_rows)
    shared = SHARED if n == 8 and layers == 4 and columns == slots == 4 and columns < local else 0
    per = local // layers if shared else 1
    chunk = shared // CHUNKS if shared else 128
    chunks = CHUNKS if shared else 1
    out = pl.pallas_call(
        functools.partial(kernel, n, layers, columns, shared, pack),
        out_shape=jax.ShapeDtypeStruct((part_rows, held_rows), jnp.float32),
        in_specs=[
            pl.BlockSpec(memory_space=pltpu.SMEM),
            pl.BlockSpec(memory_space=pl.ANY),
            pl.BlockSpec(memory_space=pl.ANY),
        ],
        out_specs=pl.BlockSpec(memory_space=pltpu.VMEM),
        scratch_shapes=[
            pltpu.SMEM((n, 1, slots), jnp.int32),
            pltpu.VMEM(amplitudes.shape, jnp.float32),
            pltpu.VMEM((slots, width, depth), jnp.float32),
            pltpu.VMEM((slots, 2 * width, depth), jnp.bfloat16),
            pltpu.VMEM((columns, n, own_rows, depth), jnp.float32),
            pltpu.VMEM((columns, n, own_rows, depth), jnp.float32),
            pltpu.VMEM((slots, n, own_rows, chunk), jnp.float32),
            pltpu.VMEM((slots, 2 * width, 2 * held_rows), jnp.float32),
            pltpu.VMEM((n, part_rows // pack, held_rows * pack), jnp.float32),
            pltpu.VMEM((n, part_rows // pack, held_rows * pack), jnp.float32),
            pltpu.SemaphoreType.DMA((2,)),
            pltpu.SemaphoreType.DMA((n,)),
            pltpu.SemaphoreType.DMA((n,)),
            pltpu.SemaphoreType.DMA((columns, n)),
            pltpu.SemaphoreType.DMA((columns, n)),
            pltpu.SemaphoreType.DMA((columns, 2)),
            pltpu.SemaphoreType.DMA((columns, 2)),
            pltpu.SemaphoreType.DMA((chunks, per, 2)),
            pltpu.SemaphoreType.DMA((chunks, per, 2)),
            pltpu.SemaphoreType.DMA((2, chunks, local)),
            pltpu.SemaphoreType.DMA((chunks, local)),
            pltpu.SemaphoreType.DMA((n,)),
            pltpu.SemaphoreType.DMA((n,)),
        ] + [pltpu.VMEM((local, 2, own_rows, chunk), jnp.float32)] * (chunks if shared else 0),
        compiler_params=pltpu.CompilerParams(
            collective_id=0, has_side_effects=True, vmem_limit_bytes=60 * 1024 * 1024),
    )(tasks[0], amplitudes, integrals[0, 0])
    return out[None]


def solution(mesh):
    return jax.shard_map(
        functools.partial(body, mesh.shape["pair"], mesh.shape["grp"]),
        mesh=mesh,
        in_specs=(
            P("pair", None, None),
            P("grp", "pair", None, None, None),
            P("grp", "pair", None),
        ),
        out_specs=P("grp", "pair", None),
        check_vma=False,
    )
```

```python
import functools

import jax
import jax.numpy as jnp
from jax import lax
from jax.experimental import pallas as pl
from jax.experimental.pallas import tpu as pltpu
from jax.sharding import PartitionSpec as P

NT = 8
CHUNKS = (512, 640, 768, 768, 768, 640)
GROUPS = (3, 1)
MESH = pl.DeviceIdType.MESH


def split(x):
    high = x.astype(jnp.bfloat16)
    low = (x - high.astype(jnp.float32)).astype(jnp.bfloat16)
    return jnp.concatenate([high, low], axis=0)


def multiply(rows, operand):
    operand = operand.reshape(-1, operand.shape[-1])
    return lax.dot_general(rows, split(operand), (((1,), (1,)), ((), ())), preferred_element_type=jnp.float32)


def tile_totals(tasks_ref, both, total, n, local, width, part_rows, pack):
    slots = both.shape[0]
    piece = part_rows // pack
    tiles, terms = [], []
    for slot in range(slots):
        code = tasks_ref[0, slot]
        tiles.append(jnp.where(code >= 0, lax.div(jnp.maximum(code, 0), local), -1))
        term = both[slot]
        term = term[:width] + term[width:]
        half = term.shape[1] // 2
        terms.append(term[:, :half] + term[:, half:])
    packed = {}
    for p in range(n):
        first = p * part_rows
        low = first % width
        value = jnp.zeros(total.shape[1:], jnp.float32)
        for slot in range(slots):
            if (slot, low) not in packed:
                packed[slot, low] = jnp.concatenate(
                    [terms[slot][low + i * piece: low + (i + 1) * piece] for i in range(pack)], axis=1)
            value += jnp.where(tiles[slot] == first // width, packed[slot, low], 0.0)
        total[p] = value


def write_sum(parts, out_ref, pack):
    n = parts.shape[0]
    piece = out_ref.shape[0] // pack
    held_rows = out_ref.shape[1]
    result = parts[0]
    for p in range(1, n):
        result += parts[p]
    for i in range(pack):
        out_ref[i * piece: (i + 1) * piece, :] = result[:, i * held_rows: (i + 1) * held_rows]


def plane_kernel(layers, pack, tasks_ref, amp_ref, int_ref, out_ref, listed, amp, blocks, rows, chosen, both, total,
                 parts, amp_sem, int_sem, list_send, list_recv, near_send, near_recv, tail_send, tail_recv, fetch_send,
                 fetch_recv, own_send, relay_send, layer_recv,
                 pick_send, pick_recv, part_send, part_recv, outer_list, outer_send, outer_recv, *buffers):
    n = 8
    me = lax.axis_index("pair")
    grp = lax.axis_index("grp")
    own_rows, pairs, depth = amp_ref.shape
    slots, width, _ = int_ref.shape
    local = pairs // n
    per = local // layers
    shared = sum(CHUNKS)
    tail = depth - shared
    sent, held = buffers[:len(GROUPS)], buffers[len(GROUPS): 2 * len(GROUPS)]
    far = buffers[2 * len(GROUPS): 2 * len(GROUPS) + len(CHUNKS)]
    used = 2 * len(GROUPS) + len(CHUNKS)
    pick_sent, pick_held = buffers[used: used + len(CHUNKS)], buffers[used + len(CHUNKS): used + 2 * len(CHUNKS)]
    tail_sent, tail_held = buffers[-2:] if tail else (None, None)
    starts = [sum(CHUNKS[:q]) for q in range(len(CHUNKS))]
    firsts = [sum(GROUPS[:g]) for g in range(len(GROUPS))]

    def bit(value, d):
        return value if not d else 1 - value

    core, x, y = lax.rem(me, 2), lax.rem(me // 2, 2), me // 4
    peer = [bit(y, d // 4) * 4 + bit(x, d // 2 % 2) * 2 + bit(core, d % 2) for d in range(n)]
    near = (2, 4, 3, 5, 1)
    distant = (6, 7)
    inner = (grp >= 1) & (grp <= 2)
    inward = lax.rem(grp, 2) + 1
    outward = (grp - 1) * 3

    def target(d):
        return (peer[d], grp)

    load_amp = pltpu.make_async_copy(amp_ref, amp, amp_sem)
    load_int = pltpu.make_async_copy(int_ref, blocks, int_sem)
    load_amp.start()

    barrier = pltpu.get_barrier_semaphore()
    for d in (6, 7, 2, 3, 4, 5, 1):
        pl.semaphore_signal(barrier, inc=1, device_id=target(d), device_id_type=MESH)

    @pl.when(grp > 0)
    def _():
        pl.semaphore_signal(barrier, inc=1, device_id=(me, grp - 1), device_id_type=MESH)

    @pl.when(grp < layers - 1)
    def _():
        pl.semaphore_signal(barrier, inc=1, device_id=(me, grp + 1), device_id_type=MESH)

    for d in distant:
        for group, size in enumerate(GROUPS):
            held[group][peer[d]] = jnp.zeros_like(held[group][peer[d]])
    chosen[...] = jnp.zeros_like(chosen)
    pl.semaphore_wait(barrier, n - 1 + jnp.minimum(grp, 1) + jnp.minimum(layers - 1 - grp, 1))

    def list_copy(d, receive=False):
        return pltpu.make_async_remote_copy(
            src_ref=tasks_ref, dst_ref=listed.at[peer[d] if receive else me], send_sem=list_send.at[d],
            recv_sem=list_recv.at[d], device_id=target(d), device_id_type=MESH)

    def near_copy(group, d, receive=False):
        return pltpu.make_async_remote_copy(
            src_ref=sent[group].at[peer[d]], dst_ref=held[group].at[peer[d] if receive else me],
            send_sem=near_send.at[group, d], recv_sem=near_recv.at[group, d], device_id=target(d),
            device_id_type=MESH)

    def tail_copy(f):
        return pltpu.make_async_remote_copy(
            src_ref=tail_sent.at[f], dst_ref=tail_held.at[f], send_sem=tail_send.at[f], recv_sem=tail_recv.at[f],
            device_id=target(distant[f]), device_id_type=MESH)

    def fetch_copy(q, j, f):
        column = peer[distant[f]] * local + grp * per + j
        return pltpu.make_async_remote_copy(
            src_ref=amp_ref.at[:, column, pl.ds(starts[q], CHUNKS[q])], dst_ref=far[q].at[grp * per + j, f],
            send_sem=fetch_send.at[q, j, f], recv_sem=fetch_recv.at[q, j, f], device_id=target(distant[f]),
            device_id_type=MESH)

    def layer_copy(block, q, send):
        at = far[q].at[pl.ds(block * per, per)]
        return pltpu.make_async_remote_copy(
            src_ref=at, dst_ref=at, send_sem=send.at[q], recv_sem=layer_recv.at[q, block], device_id=(me, inward),
            device_id_type=MESH)

    def own_copy(q):
        return layer_copy(grp, q, own_send)

    def relay_copy(q):
        return layer_copy(outward, q, relay_send)

    def pick_copy(q, to):
        return pltpu.make_async_remote_copy(
            src_ref=pick_sent[q], dst_ref=pick_held[q], send_sem=pick_send.at[q], recv_sem=pick_recv.at[q],
            device_id=(me, to), device_id_type=MESH)

    outer_copy = pltpu.make_async_remote_copy(
        src_ref=tasks_ref, dst_ref=outer_list, send_sem=outer_send, recv_sem=outer_recv, device_id=(me, inward),
        device_id_type=MESH)

    def part_copy(d, receive=False):
        return pltpu.make_async_remote_copy(
            src_ref=total.at[peer[d]], dst_ref=parts.at[peer[d] if receive else me], send_sem=part_send.at[d],
            recv_sem=part_recv.at[d], device_id=target(d), device_id_type=MESH)

    for d in range(1, n):
        list_copy(d).start()

    @pl.when(jnp.logical_not(inner))
    def _():
        outer_copy.start()

    fetches = [(j, f) for j in range(per) for f in range(len(distant))]
    for q in range(len(CHUNKS)):
        for j, f in fetches:
            fetch_copy(q, j, f).start()

    def local_pair(code):
        return lax.rem(jnp.maximum(code, 0), local)

    def column(p, slot, code):
        return p * local + local_pair(code)

    def send_near(group):
        for d in near + (0,):
            for k in range(GROUPS[group]):
                slot = firsts[group] + k
                code = listed[peer[d], 0, slot] if d else tasks_ref[0, slot]
                at = column(peer[d], slot, code)
                to = sent[group] if d else held[group]
                for row in range(own_rows):
                    to[peer[d], k, pl.ds(row, 1), :] = amp[row, pl.ds(at, 1), :]
            if d:
                near_copy(group, d).start()

    def send_tail():
        for f, d in enumerate(distant):
            for slot in range(slots):
                at = column(peer[d], slot, listed[peer[d], 0, slot])
                for row in range(own_rows):
                    tail_sent[f, slot, pl.ds(row, 1), :] = amp[row, pl.ds(at, 1), pl.ds(shared, tail)]
            tail_copy(f).start()


    def fetched(q):
        for j, f in fetches:
            fetch_copy(q, j, f).wait_recv()
        own_copy(q).start()

    def relay(q):
        @pl.when(inner)
        def _():
            relay_copy(q).wait_recv()
            relay_copy(q).start()

    def select(q):
        @pl.when(inner)
        def _():
            layer_copy(inward, q, own_send).wait_recv()
            layer_copy(3 - outward, q, own_send).wait_recv()
            for slot in range(slots):
                pick_sent[q][slot] = far[q][local_pair(outer_list[0, slot])]
            pick_copy(q, outward).start()

    def near_part(group):
        for d in near:
            near_copy(group, d, True).wait_recv()
        for k in range(GROUPS[group]):
            slot = firsts[group] + k
            both[slot] = multiply(rows[slot], held[group][:, k])

    def far_part(q):
        @pl.when(inner)
        def _():
            for slot in range(slots):
                for f, d in enumerate(distant):
                    chosen[slot, peer[d], :, :CHUNKS[q]] = far[q][local_pair(tasks_ref[0, slot]), f]

        @pl.when(jnp.logical_not(inner))
        def _():
            pick_copy(q, inward).wait_recv()
            for slot in range(slots):
                for f, d in enumerate(distant):
                    chosen[slot, peer[d], :, :CHUNKS[q]] = pick_held[q][slot, f]

        for slot in range(slots):
            both[slot] += multiply(rows[slot, :, pl.ds(starts[q], CHUNKS[q])], chosen[slot, :, :, :CHUNKS[q]])

    def tail_part():
        for f in range(len(distant)):
            tail_copy(f).wait_recv()
        for slot in range(slots):
            for f, d in enumerate(distant):
                chosen[slot, peer[d], :, :tail] = tail_held[f, slot]
            both[slot] += multiply(rows[slot, :, pl.ds(shared, tail)], chosen[slot, :, :, :tail])

    chunks = len(CHUNKS)
    last = chunks - 1

    @pl.when(inner)
    def _():
        outer_copy.wait_recv()

    fetched(0)
    load_amp.wait()
    for d in range(1, n):
        list_copy(d, True).wait_recv()
    send_near(0)
    relay(0)
    load_int.start()
    fetched(1)
    relay(1)
    select(0)
    for group in range(1, len(GROUPS)):
        send_near(group)
    if tail:
        send_tail()
    for q in range(2, chunks):
        fetched(q)
        relay(q)
        if q < last:
            select(q - 1)
    load_int.wait()

    @pl.loop(0, slots)
    def _(slot):
        rows[slot] = split(blocks[slot])

    for q in range(max(1, last - 1), chunks):
        select(q)
    for d in range(1, n):
        list_copy(d).wait_send()
    for q in range(chunks):
        for j, f in fetches:
            fetch_copy(q, j, f).wait_send()
        own_copy(q).wait_send()
    for group in range(len(GROUPS) - 1):
        near_part(group)
        for d in near:
            near_copy(group, d).wait_send()
    for slot in range(firsts[-1], slots):
        both[slot] = jnp.zeros_like(both[slot])
    for q in range(chunks):
        far_part(q)
    if tail:
        tail_part()
    for d in near:
        near_copy(len(GROUPS) - 1, d, True).wait_recv()
    for k in range(GROUPS[-1]):
        slot = firsts[-1] + k
        both[slot] += multiply(rows[slot], held[-1][:, k])

    tile_totals(tasks_ref, both, total, n, local, width, out_ref.shape[0], pack)
    for d in (6, 7, 2, 4, 3, 5, 1):
        part_copy(d).start()
    parts[me] = total[me]
    for d in near:
        near_copy(len(GROUPS) - 1, d).wait_send()
    if tail:
        for f in range(len(distant)):
            tail_copy(f).wait_send()

    @pl.when(inner)
    def _():
        for q in range(chunks):
            relay_copy(q).wait_send()
            pick_copy(q, outward).wait_send()

    @pl.when(jnp.logical_not(inner))
    def _():
        outer_copy.wait_send()

    for d in range(1, n):
        part_copy(d, True).wait_recv()
    write_sum(parts, out_ref, pack)
    for d in range(1, n):
        part_copy(d).wait_send()


def direct_kernel(n, columns, pack, tasks_ref, amp_ref, int_ref, out_ref, listed, amp, blocks, rows, sent, held, both,
                  total, parts, local_sem, list_send, list_recv, send_sem, recv_sem, part_send, part_recv):
    me = lax.axis_index("pair")
    grp = lax.axis_index("grp")
    own_rows, pairs, depth = amp_ref.shape
    slots, width, _ = int_ref.shape
    local = pairs // n
    lists = columns < local

    load_amp = pltpu.make_async_copy(amp_ref, amp, local_sem.at[0])
    load_int = pltpu.make_async_copy(int_ref, blocks, local_sem.at[1])
    load_amp.start()
    load_int.start()

    def other(d):
        return lax.rem(me + d, n)

    def target(p):
        return (p, grp)

    barrier = pltpu.get_barrier_semaphore()

    @pl.loop(1, n)
    def _(d):
        pl.semaphore_signal(barrier, inc=1, device_id=target(other(d)), device_id_type=MESH)

    pl.semaphore_wait(barrier, n - 1)

    def list_copy(frm, to):
        return pltpu.make_async_remote_copy(
            src_ref=tasks_ref, dst_ref=listed.at[frm], send_sem=list_send.at[to], recv_sem=list_recv.at[frm],
            device_id=target(to), device_id_type=MESH)

    def column_copy(c, frm, to):
        return pltpu.make_async_remote_copy(
            src_ref=sent.at[c, to], dst_ref=held.at[c, frm], send_sem=send_sem.at[c, to],
            recv_sem=recv_sem.at[c, frm], device_id=target(to), device_id_type=MESH)

    def part_copy(frm, to):
        return pltpu.make_async_remote_copy(
            src_ref=total.at[to], dst_ref=parts.at[frm], send_sem=part_send.at[to],
            recv_sem=part_recv.at[frm], device_id=target(to), device_id_type=MESH)

    if lists:
        @pl.loop(1, n)
        def _(d):
            list_copy(me, other(d)).start()

    load_amp.wait()

    if lists:
        @pl.loop(1, n)
        def _(d):
            list_copy(other(d), other(d)).wait_recv()

    def column(p, c, codes):
        if lists:
            return p * local + lax.rem(jnp.maximum(codes(c), 0), local)
        return p * local + c

    for c in range(columns):
        @pl.loop(1, n)
        def _(d):
            p = other(d)
            at = column(p, c, lambda k: listed[p, 0, k])
            for row in range(own_rows):
                sent[c, p, pl.ds(row, 1), :] = amp[row, pl.ds(at, 1), :]

            @pl.when(d > 1)
            def _():
                column_copy(c, me, other(d - 1)).start()

        at = column(me, c, lambda k: tasks_ref[0, k])
        for row in range(own_rows):
            held[c, me, pl.ds(row, 1), :] = amp[row, pl.ds(at, 1), :]
        column_copy(c, me, other(n - 1)).start()

    load_int.wait()

    @pl.loop(0, slots)
    def _(slot):
        rows[slot] = split(blocks[slot])

    def arrive(c):
        @pl.loop(1, n)
        def _(d):
            column_copy(c, other(d), other(d)).wait_recv()

    if lists:
        for slot in range(slots):
            arrive(slot)
            both[slot] = multiply(rows[slot], held[slot])
    else:
        for c in range(columns):
            arrive(c)

        @pl.loop(0, slots)
        def _(slot):
            both[slot] = multiply(rows[slot], held[lax.rem(jnp.maximum(tasks_ref[0, slot], 0), local)])

    tile_totals(tasks_ref, both, total, n, local, width, out_ref.shape[0], pack)

    @pl.loop(1, n)
    def _(d):
        part_copy(me, other(d)).start()

    parts[me] = total[me]

    @pl.loop(1, n)
    def _(d):
        part_copy(other(d), other(d)).wait_recv()

    write_sum(parts, out_ref, pack)

    @pl.loop(1, n)
    def _(d):
        part_copy(me, other(d)).wait_send()
        if lists:
            list_copy(me, other(d)).wait_send()
        for c in range(columns):
            column_copy(c, me, other(d)).wait_send()


def body(n, layers, amplitudes, integrals, tasks):
    own_rows, pairs, depth = amplitudes.shape
    slots, width = integrals.shape[2:4]
    local = pairs // n
    columns = min(local, slots)
    part_rows = NT * width // n
    held_rows = n * own_rows
    pack = max(1, 128 // held_rows)
    tail = depth - sum(CHUNKS)
    planes = n == 8 and layers == 4 and local == 8 and slots == sum(GROUPS) and tail >= 0
    dma = pltpu.SemaphoreType.DMA
    scratch = [
        pltpu.SMEM((n, 1, slots), jnp.int32),
        pltpu.VMEM(amplitudes.shape, jnp.float32),
        pltpu.VMEM((slots, width, depth), jnp.float32),
        pltpu.VMEM((slots, 2 * width, depth), jnp.bfloat16),
    ]
    results = [
        pltpu.VMEM((slots, 2 * width, 2 * held_rows), jnp.float32),
        pltpu.VMEM((n, part_rows // pack, held_rows * pack), jnp.float32),
        pltpu.VMEM((n, part_rows // pack, held_rows * pack), jnp.float32),
    ]
    if planes:
        per = local // layers
        kernel = functools.partial(plane_kernel, layers, pack)
        scratch += [pltpu.VMEM((slots, n, own_rows, max(CHUNKS + (tail,))), jnp.float32)] + results + [
            dma, dma, dma((n,)), dma((n,)), dma((len(GROUPS), n)), dma((len(GROUPS), n)), dma((2,)), dma((2,)),
            dma((len(CHUNKS), per, 2)), dma((len(CHUNKS), per, 2)), dma((len(CHUNKS),)), dma((len(CHUNKS),)),
            dma((len(CHUNKS), layers)), dma((len(CHUNKS),)), dma((len(CHUNKS),)), dma((n,)), dma((n,)),
            pltpu.SMEM((1, slots), jnp.int32), dma, dma,
        ]
        scratch += 2 * [pltpu.VMEM((n, size, own_rows, depth), jnp.float32) for size in GROUPS]
        scratch += [pltpu.VMEM((local, 2, own_rows, chunk), jnp.float32) for chunk in CHUNKS]
        scratch += 2 * [pltpu.VMEM((slots, 2, own_rows, chunk), jnp.float32) for chunk in CHUNKS]
        if tail:
            scratch += 2 * [pltpu.VMEM((2, slots, own_rows, tail), jnp.float32)]
    else:
        kernel = functools.partial(direct_kernel, n, columns, pack)
        scratch += 2 * [pltpu.VMEM((columns, n, own_rows, depth), jnp.float32)] + results + [
            dma((2,)), dma((n,)), dma((n,)), dma((columns, n)), dma((columns, n)), dma((n,)), dma((n,)),
        ]
    out = pl.pallas_call(
        kernel,
        out_shape=jax.ShapeDtypeStruct((part_rows, held_rows), jnp.float32),
        in_specs=[
            pl.BlockSpec(memory_space=pltpu.SMEM),
            pl.BlockSpec(memory_space=pl.ANY),
            pl.BlockSpec(memory_space=pl.ANY),
        ],
        out_specs=pl.BlockSpec(memory_space=pltpu.VMEM),
        scratch_shapes=scratch,
        compiler_params=pltpu.CompilerParams(
            collective_id=0, has_side_effects=True, vmem_limit_bytes=60 * 1024 * 1024),
    )(tasks[0], amplitudes, integrals[0, 0])
    return out[None]


def solution(mesh):
    return jax.shard_map(
        functools.partial(body, mesh.shape["pair"], mesh.shape["grp"]),
        mesh=mesh,
        in_specs=(
            P("pair", None, None),
            P("grp", "pair", None, None, None),
            P("grp", "pair", None),
        ),
        out_specs=P("grp", "pair", None),
        check_vma=False,
    )
```

```python
import functools

import jax
import jax.numpy as jnp
from jax import lax
from jax.experimental import pallas as pl
from jax.experimental.pallas import tpu as pltpu
from jax.sharding import PartitionSpec as P

NT = 8
CHUNKS = (512, 640, 768, 768, 768, 640)
GROUPS = (3, 1)
MESH = pl.DeviceIdType.MESH


def split(x):
    high = x.astype(jnp.bfloat16)
    low = (x - high.astype(jnp.float32)).astype(jnp.bfloat16)
    return jnp.concatenate([high, low], axis=0)


def multiply(rows, operand):
    operand = operand.reshape(-1, operand.shape[-1])
    return lax.dot_general(rows, split(operand), (((1,), (1,)), ((), ())), preferred_element_type=jnp.float32)


def tile_totals(tasks_ref, both, total, n, local, width, part_rows, pack):
    slots = both.shape[0]
    piece = part_rows // pack
    tiles, terms = [], []
    for slot in range(slots):
        code = tasks_ref[0, slot]
        tiles.append(jnp.where(code >= 0, lax.div(jnp.maximum(code, 0), local), -1))
        term = both[slot]
        term = term[:width] + term[width:]
        half = term.shape[1] // 2
        terms.append(term[:, :half] + term[:, half:])
    packed = {}
    for p in range(n):
        first = p * part_rows
        low = first % width
        value = jnp.zeros(total.shape[1:], jnp.float32)
        for slot in range(slots):
            if (slot, low) not in packed:
                packed[slot, low] = jnp.concatenate(
                    [terms[slot][low + i * piece: low + (i + 1) * piece] for i in range(pack)], axis=1)
            value += jnp.where(tiles[slot] == first // width, packed[slot, low], 0.0)
        total[p] = value


def write_sum(parts, out_ref, pack):
    n = parts.shape[0]
    piece = out_ref.shape[0] // pack
    held_rows = out_ref.shape[1]
    result = parts[0]
    for p in range(1, n):
        result += parts[p]
    for i in range(pack):
        out_ref[i * piece: (i + 1) * piece, :] = result[:, i * held_rows: (i + 1) * held_rows]


def plane_kernel(layers, pack, tasks_ref, amp_ref, int_ref, out_ref, listed, amp, blocks, rows, chosen, both, total,
                 parts, amp_sem, int_sem, list_send, list_recv, near_send, near_recv, tail_send, tail_recv, fetch_send,
                 fetch_recv, own_send, second_send, layer_recv,
                 pick_send, pick_recv, part_send, part_recv, outer_list, outer_send, outer_recv, *buffers):
    n = 8
    me = lax.axis_index("pair")
    grp = lax.axis_index("grp")
    own_rows, pairs, depth = amp_ref.shape
    slots, width, _ = int_ref.shape
    local = pairs // n
    per = local // layers
    shared = sum(CHUNKS)
    tail = depth - shared
    sent, held = buffers[:len(GROUPS)], buffers[len(GROUPS): 2 * len(GROUPS)]
    far = buffers[2 * len(GROUPS): 2 * len(GROUPS) + len(CHUNKS)]
    used = 2 * len(GROUPS) + len(CHUNKS)
    pick_sent, pick_held = buffers[used: used + len(CHUNKS)], buffers[used + len(CHUNKS): used + 2 * len(CHUNKS)]
    tail_sent, tail_held = buffers[-2:] if tail else (None, None)
    starts = [sum(CHUNKS[:q]) for q in range(len(CHUNKS))]
    firsts = [sum(GROUPS[:g]) for g in range(len(GROUPS))]

    def bit(value, d):
        return value if not d else 1 - value

    core, x, y = lax.rem(me, 2), lax.rem(me // 2, 2), me // 4
    peer = [bit(y, d // 4) * 4 + bit(x, d // 2 % 2) * 2 + bit(core, d % 2) for d in range(n)]
    near = (2, 4, 3, 5, 1)
    distant = (6, 7)
    inner = (grp >= 1) & (grp <= 2)
    inward = lax.rem(grp, 2) + 1
    outward = (grp - 1) * 3
    second = jnp.where(inner, 3 - outward, 3 - inward)

    def target(d):
        return (peer[d], grp)

    load_amp = pltpu.make_async_copy(amp_ref, amp, amp_sem)
    load_int = pltpu.make_async_copy(int_ref, blocks, int_sem)
    load_amp.start()

    barrier = pltpu.get_barrier_semaphore()
    for d in (6, 7, 2, 3, 4, 5, 1):
        pl.semaphore_signal(barrier, inc=1, device_id=target(d), device_id_type=MESH)

    pl.semaphore_signal(barrier, inc=1, device_id=(me, inward), device_id_type=MESH)
    pl.semaphore_signal(barrier, inc=1, device_id=(me, second), device_id_type=MESH)

    @pl.when(inner)
    def _():
        pl.semaphore_signal(barrier, inc=1, device_id=(me, outward), device_id_type=MESH)

    for d in distant:
        for group, size in enumerate(GROUPS):
            held[group][peer[d]] = jnp.zeros_like(held[group][peer[d]])
    chosen[...] = jnp.zeros_like(chosen)
    pl.semaphore_wait(barrier, n + 1 + jnp.where(inner, 1, 0))

    def list_copy(d, receive=False):
        return pltpu.make_async_remote_copy(
            src_ref=tasks_ref, dst_ref=listed.at[peer[d] if receive else me], send_sem=list_send.at[d],
            recv_sem=list_recv.at[d], device_id=target(d), device_id_type=MESH)

    def near_copy(group, d, receive=False):
        return pltpu.make_async_remote_copy(
            src_ref=sent[group].at[peer[d]], dst_ref=held[group].at[peer[d] if receive else me],
            send_sem=near_send.at[group, d], recv_sem=near_recv.at[group, d], device_id=target(d),
            device_id_type=MESH)

    def tail_copy(f):
        return pltpu.make_async_remote_copy(
            src_ref=tail_sent.at[f], dst_ref=tail_held.at[f], send_sem=tail_send.at[f], recv_sem=tail_recv.at[f],
            device_id=target(distant[f]), device_id_type=MESH)

    def fetch_copy(q, j, f):
        column = peer[distant[f]] * local + grp * per + j
        return pltpu.make_async_remote_copy(
            src_ref=amp_ref.at[:, column, pl.ds(starts[q], CHUNKS[q])], dst_ref=far[q].at[grp * per + j, f],
            send_sem=fetch_send.at[q, j, f], recv_sem=fetch_recv.at[q, j, f], device_id=target(distant[f]),
            device_id_type=MESH)

    def layer_copy(block, q, send, to):
        at = far[q].at[pl.ds(block * per, per)]
        return pltpu.make_async_remote_copy(
            src_ref=at, dst_ref=at, send_sem=send.at[q], recv_sem=layer_recv.at[q, block], device_id=(me, to),
            device_id_type=MESH)

    def own_copy(q):
        return layer_copy(grp, q, own_send, inward)

    def second_copy(q):
        return layer_copy(grp, q, second_send, second)

    def pick_copy(q, to):
        return pltpu.make_async_remote_copy(
            src_ref=pick_sent[q], dst_ref=pick_held[q], send_sem=pick_send.at[q], recv_sem=pick_recv.at[q],
            device_id=(me, to), device_id_type=MESH)

    outer_copy = pltpu.make_async_remote_copy(
        src_ref=tasks_ref, dst_ref=outer_list, send_sem=outer_send, recv_sem=outer_recv, device_id=(me, inward),
        device_id_type=MESH)

    def part_copy(d, receive=False):
        return pltpu.make_async_remote_copy(
            src_ref=total.at[peer[d]], dst_ref=parts.at[peer[d] if receive else me], send_sem=part_send.at[d],
            recv_sem=part_recv.at[d], device_id=target(d), device_id_type=MESH)

    fetches = [(j, f) for j in range(per) for f in range(len(distant))]
    for j, f in fetches:
        fetch_copy(0, j, f).start()
    for d in range(1, n):
        list_copy(d).start()

    @pl.when(jnp.logical_not(inner))
    def _():
        outer_copy.start()

    for q in range(1, len(CHUNKS)):
        for j, f in fetches:
            fetch_copy(q, j, f).start()

    def local_pair(code):
        return lax.rem(jnp.maximum(code, 0), local)

    def column(p, slot, code):
        return p * local + local_pair(code)

    pieces = [(group, d) for group in range(len(GROUPS)) for d in near + (0,)]

    def send_near(count):
        for group, d in pieces[:count]:
            for k in range(GROUPS[group]):
                slot = firsts[group] + k
                code = listed[peer[d], 0, slot] if d else tasks_ref[0, slot]
                at = column(peer[d], slot, code)
                to = sent[group] if d else held[group]
                for row in range(own_rows):
                    to[peer[d], k, pl.ds(row, 1), :] = amp[row, pl.ds(at, 1), :]
            if d:
                near_copy(group, d).start()
        del pieces[:count]

    def send_tail():
        for f, d in enumerate(distant):
            for slot in range(slots):
                at = column(peer[d], slot, listed[peer[d], 0, slot])
                for row in range(own_rows):
                    tail_sent[f, slot, pl.ds(row, 1), :] = amp[row, pl.ds(at, 1), pl.ds(shared, tail)]
            tail_copy(f).start()


    def fetched(q):
        for j, f in fetches:
            fetch_copy(q, j, f).wait_recv()

        @pl.when(jnp.logical_not(inner))
        def _():
            second_copy(q).start()

        own_copy(q).start()

    def select(q):
        @pl.when(inner)
        def _():
            for block in (outward, inward, second):
                layer_copy(block, q, own_send, inward).wait_recv()
            for slot in range(slots):
                pick_sent[q][slot] = far[q][local_pair(outer_list[0, slot])]
            pick_copy(q, outward).start()

    def near_part(group):
        for d in near:
            near_copy(group, d, True).wait_recv()
        for k in range(GROUPS[group]):
            slot = firsts[group] + k
            both[slot] = multiply(rows[slot], held[group][:, k])

    def far_part(q):
        @pl.when(inner)
        def _():
            for slot in range(slots):
                for f, d in enumerate(distant):
                    chosen[slot, peer[d], :, :CHUNKS[q]] = far[q][local_pair(tasks_ref[0, slot]), f]

        @pl.when(jnp.logical_not(inner))
        def _():
            pick_copy(q, inward).wait_recv()
            for slot in range(slots):
                for f, d in enumerate(distant):
                    chosen[slot, peer[d], :, :CHUNKS[q]] = pick_held[q][slot, f]

        for slot in range(slots):
            both[slot] += multiply(rows[slot, :, pl.ds(starts[q], CHUNKS[q])], chosen[slot, :, :, :CHUNKS[q]])

    def tail_part():
        for f in range(len(distant)):
            tail_copy(f).wait_recv()
        for slot in range(slots):
            for f, d in enumerate(distant):
                chosen[slot, peer[d], :, :tail] = tail_held[f, slot]
            both[slot] += multiply(rows[slot, :, pl.ds(shared, tail)], chosen[slot, :, :, :tail])

    chunks = len(CHUNKS)
    last = chunks - 1

    @pl.when(inner)
    def _():
        outer_copy.wait_recv()

    fetched(0)
    load_amp.wait()
    for d in range(1, n):
        list_copy(d, True).wait_recv()
    send_near(2)
    fetched(1)
    send_near(2)
    select(0)
    load_int.start()
    for q in range(2, chunks):
        send_near(2)
        fetched(q)
        if q == 2 and tail:
            send_tail()
        if q < last:
            select(q - 1)
    send_near(len(pieces))
    load_int.wait()

    @pl.loop(0, slots)
    def _(slot):
        rows[slot] = split(blocks[slot])

    for q in range(max(1, last - 1), chunks):
        select(q)
    for d in range(1, n):
        list_copy(d).wait_send()
    for q in range(chunks):
        for j, f in fetches:
            fetch_copy(q, j, f).wait_send()
        own_copy(q).wait_send()
    for group in range(len(GROUPS) - 1):
        near_part(group)
        for d in near:
            near_copy(group, d).wait_send()
    for slot in range(firsts[-1], slots):
        both[slot] = jnp.zeros_like(both[slot])
    for q in range(chunks):
        far_part(q)
    if tail:
        tail_part()
    for d in near:
        near_copy(len(GROUPS) - 1, d, True).wait_recv()
    for k in range(GROUPS[-1]):
        slot = firsts[-1] + k
        both[slot] += multiply(rows[slot], held[-1][:, k])

    tile_totals(tasks_ref, both, total, n, local, width, out_ref.shape[0], pack)
    for d in (6, 7, 2, 4, 3, 5, 1):
        part_copy(d).start()
    parts[me] = total[me]
    for d in near:
        near_copy(len(GROUPS) - 1, d).wait_send()
    if tail:
        for f in range(len(distant)):
            tail_copy(f).wait_send()

    @pl.when(inner)
    def _():
        for q in range(chunks):
            pick_copy(q, outward).wait_send()

    @pl.when(jnp.logical_not(inner))
    def _():
        outer_copy.wait_send()
        for q in range(chunks):
            second_copy(q).wait_send()

    for d in range(1, n):
        part_copy(d, True).wait_recv()
    write_sum(parts, out_ref, pack)
    for d in range(1, n):
        part_copy(d).wait_send()


def direct_kernel(n, columns, pack, tasks_ref, amp_ref, int_ref, out_ref, listed, amp, blocks, rows, sent, held, both,
                  total, parts, local_sem, list_send, list_recv, send_sem, recv_sem, part_send, part_recv):
    me = lax.axis_index("pair")
    grp = lax.axis_index("grp")
    own_rows, pairs, depth = amp_ref.shape
    slots, width, _ = int_ref.shape
    local = pairs // n
    lists = columns < local

    load_amp = pltpu.make_async_copy(amp_ref, amp, local_sem.at[0])
    load_int = pltpu.make_async_copy(int_ref, blocks, local_sem.at[1])
    load_amp.start()
    load_int.start()

    def other(d):
        return lax.rem(me + d, n)

    def target(p):
        return (p, grp)

    barrier = pltpu.get_barrier_semaphore()

    @pl.loop(1, n)
    def _(d):
        pl.semaphore_signal(barrier, inc=1, device_id=target(other(d)), device_id_type=MESH)

    pl.semaphore_wait(barrier, n - 1)

    def list_copy(frm, to):
        return pltpu.make_async_remote_copy(
            src_ref=tasks_ref, dst_ref=listed.at[frm], send_sem=list_send.at[to], recv_sem=list_recv.at[frm],
            device_id=target(to), device_id_type=MESH)

    def column_copy(c, frm, to):
        return pltpu.make_async_remote_copy(
            src_ref=sent.at[c, to], dst_ref=held.at[c, frm], send_sem=send_sem.at[c, to],
            recv_sem=recv_sem.at[c, frm], device_id=target(to), device_id_type=MESH)

    def part_copy(frm, to):
        return pltpu.make_async_remote_copy(
            src_ref=total.at[to], dst_ref=parts.at[frm], send_sem=part_send.at[to],
            recv_sem=part_recv.at[frm], device_id=target(to), device_id_type=MESH)

    if lists:
        @pl.loop(1, n)
        def _(d):
            list_copy(me, other(d)).start()

    load_amp.wait()

    if lists:
        @pl.loop(1, n)
        def _(d):
            list_copy(other(d), other(d)).wait_recv()

    def column(p, c, codes):
        if lists:
            return p * local + lax.rem(jnp.maximum(codes(c), 0), local)
        return p * local + c

    for c in range(columns):
        @pl.loop(1, n)
        def _(d):
            p = other(d)
            at = column(p, c, lambda k: listed[p, 0, k])
            for row in range(own_rows):
                sent[c, p, pl.ds(row, 1), :] = amp[row, pl.ds(at, 1), :]

            @pl.when(d > 1)
            def _():
                column_copy(c, me, other(d - 1)).start()

        at = column(me, c, lambda k: tasks_ref[0, k])
        for row in range(own_rows):
            held[c, me, pl.ds(row, 1), :] = amp[row, pl.ds(at, 1), :]
        column_copy(c, me, other(n - 1)).start()

    load_int.wait()

    @pl.loop(0, slots)
    def _(slot):
        rows[slot] = split(blocks[slot])

    def arrive(c):
        @pl.loop(1, n)
        def _(d):
            column_copy(c, other(d), other(d)).wait_recv()

    if lists:
        for slot in range(slots):
            arrive(slot)
            both[slot] = multiply(rows[slot], held[slot])
    else:
        for c in range(columns):
            arrive(c)

        @pl.loop(0, slots)
        def _(slot):
            both[slot] = multiply(rows[slot], held[lax.rem(jnp.maximum(tasks_ref[0, slot], 0), local)])

    tile_totals(tasks_ref, both, total, n, local, width, out_ref.shape[0], pack)

    @pl.loop(1, n)
    def _(d):
        part_copy(me, other(d)).start()

    parts[me] = total[me]

    @pl.loop(1, n)
    def _(d):
        part_copy(other(d), other(d)).wait_recv()

    write_sum(parts, out_ref, pack)

    @pl.loop(1, n)
    def _(d):
        part_copy(me, other(d)).wait_send()
        if lists:
            list_copy(me, other(d)).wait_send()
        for c in range(columns):
            column_copy(c, me, other(d)).wait_send()


def body(n, layers, amplitudes, integrals, tasks):
    own_rows, pairs, depth = amplitudes.shape
    slots, width = integrals.shape[2:4]
    local = pairs // n
    columns = min(local, slots)
    part_rows = NT * width // n
    held_rows = n * own_rows
    pack = max(1, 128 // held_rows)
    tail = depth - sum(CHUNKS)
    planes = n == 8 and layers == 4 and local == 8 and slots == sum(GROUPS) and tail >= 0
    dma = pltpu.SemaphoreType.DMA
    scratch = [
        pltpu.SMEM((n, 1, slots), jnp.int32),
        pltpu.VMEM(amplitudes.shape, jnp.float32),
        pltpu.VMEM((slots, width, depth), jnp.float32),
        pltpu.VMEM((slots, 2 * width, depth), jnp.bfloat16),
    ]
    results = [
        pltpu.VMEM((slots, 2 * width, 2 * held_rows), jnp.float32),
        pltpu.VMEM((n, part_rows // pack, held_rows * pack), jnp.float32),
        pltpu.VMEM((n, part_rows // pack, held_rows * pack), jnp.float32),
    ]
    if planes:
        per = local // layers
        kernel = functools.partial(plane_kernel, layers, pack)
        scratch += [pltpu.VMEM((slots, n, own_rows, max(CHUNKS + (tail,))), jnp.float32)] + results + [
            dma, dma, dma((n,)), dma((n,)), dma((len(GROUPS), n)), dma((len(GROUPS), n)), dma((2,)), dma((2,)),
            dma((len(CHUNKS), per, 2)), dma((len(CHUNKS), per, 2)), dma((len(CHUNKS),)), dma((len(CHUNKS),)),
            dma((len(CHUNKS), layers)), dma((len(CHUNKS),)), dma((len(CHUNKS),)), dma((n,)), dma((n,)),
            pltpu.SMEM((1, slots), jnp.int32), dma, dma,
        ]
        scratch += 2 * [pltpu.VMEM((n, size, own_rows, depth), jnp.float32) for size in GROUPS]
        scratch += [pltpu.VMEM((local, 2, own_rows, chunk), jnp.float32) for chunk in CHUNKS]
        scratch += 2 * [pltpu.VMEM((slots, 2, own_rows, chunk), jnp.float32) for chunk in CHUNKS]
        if tail:
            scratch += 2 * [pltpu.VMEM((2, slots, own_rows, tail), jnp.float32)]
    else:
        kernel = functools.partial(direct_kernel, n, columns, pack)
        scratch += 2 * [pltpu.VMEM((columns, n, own_rows, depth), jnp.float32)] + results + [
            dma((2,)), dma((n,)), dma((n,)), dma((columns, n)), dma((columns, n)), dma((n,)), dma((n,)),
        ]
    out = pl.pallas_call(
        kernel,
        out_shape=jax.ShapeDtypeStruct((part_rows, held_rows), jnp.float32),
        in_specs=[
            pl.BlockSpec(memory_space=pltpu.SMEM),
            pl.BlockSpec(memory_space=pl.ANY),
            pl.BlockSpec(memory_space=pl.ANY),
        ],
        out_specs=pl.BlockSpec(memory_space=pltpu.VMEM),
        scratch_shapes=scratch,
        compiler_params=pltpu.CompilerParams(
            collective_id=0, has_side_effects=True, vmem_limit_bytes=60 * 1024 * 1024),
    )(tasks[0], amplitudes, integrals[0, 0])
    return out[None]


def solution(mesh):
    return jax.shard_map(
        functools.partial(body, mesh.shape["pair"], mesh.shape["grp"]),
        mesh=mesh,
        in_specs=(
            P("pair", None, None),
            P("grp", "pair", None, None, None),
            P("grp", "pair", None),
        ),
        out_specs=P("grp", "pair", None),
        check_vma=False,
    )
```

```python
import functools

import jax
import jax.numpy as jnp
from jax import lax
from jax.experimental import pallas as pl
from jax.experimental.pallas import tpu as pltpu
from jax.sharding import PartitionSpec as P

NT = 8
CHUNKS = (512, 640, 768, 768, 768, 640)
GROUPS = ((0, 3, 0, 1), (3, 1, 0, 2), (3, 1, 1, 2))
KEEP = 1
MESH = pl.DeviceIdType.MESH


def split(x):
    high = x.astype(jnp.bfloat16)
    low = (x - high.astype(jnp.float32)).astype(jnp.bfloat16)
    return jnp.concatenate([high, low], axis=0)


def multiply(rows, operand):
    operand = operand.reshape(-1, operand.shape[-1])
    return lax.dot_general(rows, split(operand), (((1,), (1,)), ((), ())), preferred_element_type=jnp.float32)


def tile_totals(tasks_ref, both, total, n, local, width, part_rows, pack, chosen_slots, more=False):
    piece = part_rows // pack
    tiles, terms = {}, {}
    for slot in chosen_slots:
        code = tasks_ref[0, slot]
        tiles[slot] = jnp.where(code >= 0, lax.div(jnp.maximum(code, 0), local), -1)
        term = both[slot]
        term = term[:width] + term[width:]
        half = term.shape[1] // 2
        terms[slot] = term[:, :half] + term[:, half:]
    packed = {}
    for p in range(n):
        first = p * part_rows
        low = first % width
        value = total[p] if more else jnp.zeros(total.shape[1:], jnp.float32)
        for slot in chosen_slots:
            if (slot, low) not in packed:
                packed[slot, low] = jnp.concatenate(
                    [terms[slot][low + i * piece: low + (i + 1) * piece] for i in range(pack)], axis=1)
            value += jnp.where(tiles[slot] == first // width, packed[slot, low], 0.0)
        total[p] = value


def write_sum(parts, out_ref, pack):
    n = parts.shape[0]
    piece = out_ref.shape[0] // pack
    held_rows = out_ref.shape[1]
    result = parts[0]
    for p in range(1, n):
        result += parts[p]
    for i in range(pack):
        out_ref[i * piece: (i + 1) * piece, :] = result[:, i * held_rows: (i + 1) * held_rows]


def plane_kernel(layers, pack, tasks_ref, amp_ref, int_ref, out_ref, listed, amp, blocks, rows, chosen, both, total,
                 parts, amp_sem, int_sem, list_send, list_recv, near_send, near_recv, tail_send, tail_recv, fetch_send,
                 fetch_recv, own_send, second_send, layer_recv,
                 pick_send, pick_recv, part_send, part_recv, outer_list, outer_send, outer_recv, *buffers):
    n = 8
    me = lax.axis_index("pair")
    grp = lax.axis_index("grp")
    own_rows, pairs, depth = amp_ref.shape
    slots, width, _ = int_ref.shape
    local = pairs // n
    per = local // layers
    shared = sum(CHUNKS)
    tail = depth - shared
    sent, held = buffers[:len(GROUPS)], buffers[len(GROUPS): 2 * len(GROUPS)]
    far = buffers[2 * len(GROUPS): 2 * len(GROUPS) + len(CHUNKS)]
    used = 2 * len(GROUPS) + len(CHUNKS)
    pick_sent, pick_held = buffers[used: used + len(CHUNKS)], buffers[used + len(CHUNKS): used + 2 * len(CHUNKS)]
    tail_sent, tail_held = buffers[-2:] if tail else (None, None)
    starts = [sum(CHUNKS[:q]) for q in range(len(CHUNKS))]
    spans = [pl.ds(part * depth // parts_of, depth // parts_of) for _, _, part, parts_of in GROUPS]

    def bit(value, d):
        return value if not d else 1 - value

    core, x, y = lax.rem(me, 2), lax.rem(me // 2, 2), me // 4
    peer = [bit(y, d // 4) * 4 + bit(x, d // 2 % 2) * 2 + bit(core, d % 2) for d in range(n)]
    near = (2, 4, 3, 5, 1)
    distant = (6, 7)
    inner = (grp >= 1) & (grp <= 2)
    inward = lax.rem(grp, 2) + 1
    outward = (grp - 1) * 3
    second = jnp.where(inner, 3 - outward, 3 - inward)

    def target(d):
        return (peer[d], grp)

    load_amp = pltpu.make_async_copy(amp_ref, amp, amp_sem)
    load_int = pltpu.make_async_copy(int_ref, blocks, int_sem)
    load_amp.start()

    barrier = pltpu.get_barrier_semaphore()
    for d in (6, 7, 2, 3, 4, 5, 1):
        pl.semaphore_signal(barrier, inc=1, device_id=target(d), device_id_type=MESH)

    pl.semaphore_signal(barrier, inc=1, device_id=(me, inward), device_id_type=MESH)
    pl.semaphore_signal(barrier, inc=1, device_id=(me, second), device_id_type=MESH)

    @pl.when(inner)
    def _():
        pl.semaphore_signal(barrier, inc=1, device_id=(me, outward), device_id_type=MESH)

    pl.semaphore_wait(barrier, n + 1 + jnp.where(inner, 1, 0))

    def list_copy(d, receive=False):
        return pltpu.make_async_remote_copy(
            src_ref=tasks_ref, dst_ref=listed.at[peer[d] if receive else me], send_sem=list_send.at[d],
            recv_sem=list_recv.at[d], device_id=target(d), device_id_type=MESH)

    def near_copy(group, d, receive=False):
        return pltpu.make_async_remote_copy(
            src_ref=sent[group].at[peer[d]], dst_ref=held[group].at[peer[d] if receive else me],
            send_sem=near_send.at[group, d], recv_sem=near_recv.at[group, d], device_id=target(d),
            device_id_type=MESH)

    def tail_copy(f):
        return pltpu.make_async_remote_copy(
            src_ref=tail_sent.at[f], dst_ref=tail_held.at[f], send_sem=tail_send.at[f], recv_sem=tail_recv.at[f],
            device_id=target(distant[f]), device_id_type=MESH)

    def fetch_copy(q, j, f):
        column = peer[distant[f]] * local + grp * per + j
        return pltpu.make_async_remote_copy(
            src_ref=amp_ref.at[:, column, pl.ds(starts[q], CHUNKS[q])], dst_ref=far[q].at[grp * per + j, f],
            send_sem=fetch_send.at[q, j, f], recv_sem=fetch_recv.at[q, j, f], device_id=target(distant[f]),
            device_id_type=MESH)

    def layer_copy(block, q, send, to):
        at = far[q].at[pl.ds(block * per, per)]
        return pltpu.make_async_remote_copy(
            src_ref=at, dst_ref=at, send_sem=send.at[q], recv_sem=layer_recv.at[q, block], device_id=(me, to),
            device_id_type=MESH)

    def own_copy(q):
        return layer_copy(grp, q, own_send, inward)

    def second_copy(q):
        return layer_copy(grp, q, second_send, second)

    def pick_copy(q, to):
        return pltpu.make_async_remote_copy(
            src_ref=pick_sent[q], dst_ref=pick_held[q], send_sem=pick_send.at[q], recv_sem=pick_recv.at[q],
            device_id=(me, to), device_id_type=MESH)

    outer_copy = pltpu.make_async_remote_copy(
        src_ref=tasks_ref, dst_ref=outer_list, send_sem=outer_send, recv_sem=outer_recv, device_id=(me, inward),
        device_id_type=MESH)

    def part_copy(d, receive=False):
        return pltpu.make_async_remote_copy(
            src_ref=total.at[peer[d]], dst_ref=parts.at[peer[d] if receive else me], send_sem=part_send.at[d],
            recv_sem=part_recv.at[d], device_id=target(d), device_id_type=MESH)

    fetches = [(j, f) for j in range(per) for f in range(len(distant))]
    for j, f in fetches:
        fetch_copy(0, j, f).start()
    for d in range(1, n):
        list_copy(d).start()

    @pl.when(jnp.logical_not(inner))
    def _():
        outer_copy.start()

    for q in range(1, len(CHUNKS)):
        for j, f in fetches:
            fetch_copy(q, j, f).start()

    for d in distant:
        for group in range(len(GROUPS)):
            held[group][peer[d]] = jnp.zeros_like(held[group][peer[d]])
    chosen[...] = jnp.zeros_like(chosen)
    both[...] = jnp.zeros_like(both)
    def local_pair(code):
        return lax.rem(jnp.maximum(code, 0), local)

    def column(p, slot, code):
        return p * local + local_pair(code)

    pieces = [(group, d) for group in range(len(GROUPS)) for d in near + (0,)]

    def send_near(count):
        for group, d in pieces[:count]:
            for k in range(GROUPS[group][1]):
                slot = GROUPS[group][0] + k
                code = listed[peer[d], 0, slot] if d else tasks_ref[0, slot]
                at = column(peer[d], slot, code)
                to = sent[group] if d else held[group]
                for row in range(own_rows):
                    to[peer[d], k, pl.ds(row, 1), :] = amp[row, pl.ds(at, 1), spans[group]]
            if d:
                near_copy(group, d).start()
        del pieces[:count]

    def send_tail():
        for f, d in enumerate(distant):
            for slot in range(slots):
                at = column(peer[d], slot, listed[peer[d], 0, slot])
                for row in range(own_rows):
                    tail_sent[f, slot, pl.ds(row, 1), :] = amp[row, pl.ds(at, 1), pl.ds(shared, tail)]
            tail_copy(f).start()


    def fetched(q):
        for j, f in fetches:
            fetch_copy(q, j, f).wait_recv()

        @pl.when(jnp.logical_not(inner))
        def _():
            second_copy(q).start()

        own_copy(q).start()

    def select(q):
        @pl.when(inner)
        def _():
            for block in (outward, inward, second):
                layer_copy(block, q, own_send, inward).wait_recv()
            for slot in range(slots):
                pick_sent[q][slot] = far[q][local_pair(outer_list[0, slot])]
            pick_copy(q, outward).start()

    def near_part(group):
        for d in near:
            near_copy(group, d, True).wait_recv()
        for k in range(GROUPS[group][1]):
            slot = GROUPS[group][0] + k
            both[slot] += multiply(rows[slot, :, spans[group]], held[group][:, k])

    def far_part(q):
        @pl.when(inner)
        def _():
            for slot in range(slots):
                for f, d in enumerate(distant):
                    chosen[slot, peer[d], :, :CHUNKS[q]] = far[q][local_pair(tasks_ref[0, slot]), f]

        @pl.when(jnp.logical_not(inner))
        def _():
            pick_copy(q, inward).wait_recv()
            for slot in range(slots):
                for f, d in enumerate(distant):
                    chosen[slot, peer[d], :, :CHUNKS[q]] = pick_held[q][slot, f]

        for slot in range(slots):
            both[slot] += multiply(rows[slot, :, pl.ds(starts[q], CHUNKS[q])], chosen[slot, :, :, :CHUNKS[q]])

    def tail_part():
        for f in range(len(distant)):
            tail_copy(f).wait_recv()
        for slot in range(slots):
            for f, d in enumerate(distant):
                chosen[slot, peer[d], :, :tail] = tail_held[f, slot]
            both[slot] += multiply(rows[slot, :, pl.ds(shared, tail)], chosen[slot, :, :, :tail])

    chunks = len(CHUNKS)
    last = chunks - 1

    @pl.when(inner)
    def _():
        outer_copy.wait_recv()

    fetched(0)
    load_amp.wait()
    for d in range(1, n):
        list_copy(d, True).wait_recv()
    send_near(2)
    fetched(1)
    send_near(2)
    select(0)
    load_int.start()
    for q in range(2, chunks):
        send_near(2)
        fetched(q)
        if q == 2 and tail:
            send_tail()
        if q < last:
            select(q - 1)
    send_near(len(pieces))
    load_int.wait()

    @pl.loop(0, slots)
    def _(slot):
        rows[slot] = split(blocks[slot])

    for q in range(max(1, last - 1), chunks):
        select(q)
    for d in range(1, n):
        list_copy(d).wait_send()
    for q in range(chunks):
        for j, f in fetches:
            fetch_copy(q, j, f).wait_send()
        own_copy(q).wait_send()
    near_part(0)
    for q in range(chunks):
        far_part(q)
    if tail:
        tail_part()
    totals = functools.partial(tile_totals, tasks_ref, both, total, n, local, width, out_ref.shape[0], pack)
    last_slot = GROUPS[-1][0]
    totals(range(last_slot))
    for d in near:
        near_copy(0, d).wait_send()
    for group in range(1, len(GROUPS)):
        near_part(group)
    totals(range(last_slot, slots), True)
    for d in (6, 7, 2, 4, 3, 5, 1):
        part_copy(d).start()
    parts[me] = total[me]
    for group in range(1, len(GROUPS)):
        for d in near:
            near_copy(group, d).wait_send()
    if tail:
        for f in range(len(distant)):
            tail_copy(f).wait_send()

    @pl.when(inner)
    def _():
        for q in range(chunks):
            pick_copy(q, outward).wait_send()

    @pl.when(jnp.logical_not(inner))
    def _():
        outer_copy.wait_send()
        for q in range(chunks):
            second_copy(q).wait_send()

    for d in (1, 2, 4, 3, 5, 6, 7):
        part_copy(d).wait_send()
    for d in (1, 2, 4, 3, 5, 6, 7):
        part_copy(d, True).wait_recv()
    write_sum(parts, out_ref, pack)


def direct_kernel(n, columns, pack, tasks_ref, amp_ref, int_ref, out_ref, listed, amp, blocks, rows, sent, held, both,
                  total, parts, local_sem, list_send, list_recv, send_sem, recv_sem, part_send, part_recv):
    me = lax.axis_index("pair")
    grp = lax.axis_index("grp")
    own_rows, pairs, depth = amp_ref.shape
    slots, width, _ = int_ref.shape
    local = pairs // n
    lists = columns < local

    load_amp = pltpu.make_async_copy(amp_ref, amp, local_sem.at[0])
    load_int = pltpu.make_async_copy(int_ref, blocks, local_sem.at[1])
    load_amp.start()
    load_int.start()

    def other(d):
        return lax.rem(me + d, n)

    def target(p):
        return (p, grp)

    barrier = pltpu.get_barrier_semaphore()

    @pl.loop(1, n)
    def _(d):
        pl.semaphore_signal(barrier, inc=1, device_id=target(other(d)), device_id_type=MESH)

    pl.semaphore_wait(barrier, n - 1)

    def list_copy(frm, to):
        return pltpu.make_async_remote_copy(
            src_ref=tasks_ref, dst_ref=listed.at[frm], send_sem=list_send.at[to], recv_sem=list_recv.at[frm],
            device_id=target(to), device_id_type=MESH)

    def column_copy(c, frm, to):
        return pltpu.make_async_remote_copy(
            src_ref=sent.at[c, to], dst_ref=held.at[c, frm], send_sem=send_sem.at[c, to],
            recv_sem=recv_sem.at[c, frm], device_id=target(to), device_id_type=MESH)

    def part_copy(frm, to):
        return pltpu.make_async_remote_copy(
            src_ref=total.at[to], dst_ref=parts.at[frm], send_sem=part_send.at[to],
            recv_sem=part_recv.at[frm], device_id=target(to), device_id_type=MESH)

    if lists:
        @pl.loop(1, n)
        def _(d):
            list_copy(me, other(d)).start()

    load_amp.wait()

    if lists:
        @pl.loop(1, n)
        def _(d):
            list_copy(other(d), other(d)).wait_recv()

    def column(p, c, codes):
        if lists:
            return p * local + lax.rem(jnp.maximum(codes(c), 0), local)
        return p * local + c

    for c in range(columns):
        @pl.loop(1, n)
        def _(d):
            p = other(d)
            at = column(p, c, lambda k: listed[p, 0, k])
            for row in range(own_rows):
                sent[c, p, pl.ds(row, 1), :] = amp[row, pl.ds(at, 1), :]

            @pl.when(d > 1)
            def _():
                column_copy(c, me, other(d - 1)).start()

        at = column(me, c, lambda k: tasks_ref[0, k])
        for row in range(own_rows):
            held[c, me, pl.ds(row, 1), :] = amp[row, pl.ds(at, 1), :]
        column_copy(c, me, other(n - 1)).start()

    load_int.wait()

    @pl.loop(0, slots)
    def _(slot):
        rows[slot] = split(blocks[slot])

    def arrive(c):
        @pl.loop(1, n)
        def _(d):
            column_copy(c, other(d), other(d)).wait_recv()

    if lists:
        for slot in range(slots):
            arrive(slot)
            both[slot] = multiply(rows[slot], held[slot])
    else:
        for c in range(columns):
            arrive(c)

        @pl.loop(0, slots)
        def _(slot):
            both[slot] = multiply(rows[slot], held[lax.rem(jnp.maximum(tasks_ref[0, slot], 0), local)])

    tile_totals(tasks_ref, both, total, n, local, width, out_ref.shape[0], pack, range(slots))

    @pl.loop(1, n)
    def _(d):
        part_copy(me, other(d)).start()

    parts[me] = total[me]

    @pl.loop(1, n)
    def _(d):
        part_copy(other(d), other(d)).wait_recv()

    write_sum(parts, out_ref, pack)

    @pl.loop(1, n)
    def _(d):
        part_copy(me, other(d)).wait_send()
        if lists:
            list_copy(me, other(d)).wait_send()
        for c in range(columns):
            column_copy(c, me, other(d)).wait_send()


def body(n, layers, amplitudes, integrals, tasks):
    own_rows, pairs, depth = amplitudes.shape
    slots, width = integrals.shape[2:4]
    local = pairs // n
    columns = min(local, slots)
    part_rows = NT * width // n
    held_rows = n * own_rows
    pack = max(1, 128 // held_rows)
    tail = depth - sum(CHUNKS)
    planes = n == 8 and layers == 4 and local == 8 and slots == 4 and tail >= 0
    dma = pltpu.SemaphoreType.DMA
    scratch = [
        pltpu.SMEM((n, 1, slots), jnp.int32),
        pltpu.VMEM(amplitudes.shape, jnp.float32),
        pltpu.VMEM((slots, width, depth), jnp.float32),
        pltpu.VMEM((slots, 2 * width, depth), jnp.bfloat16),
    ]
    results = [
        pltpu.VMEM((slots, 2 * width, 2 * held_rows), jnp.float32),
        pltpu.VMEM((n, part_rows // pack, held_rows * pack), jnp.float32),
        pltpu.VMEM((n, part_rows // pack, held_rows * pack), jnp.float32),
    ]
    if planes:
        per = local // layers
        kernel = functools.partial(plane_kernel, layers, pack)
        scratch += [pltpu.VMEM((slots, n, own_rows, max(CHUNKS + (tail,))), jnp.float32)] + results + [
            dma, dma, dma((n,)), dma((n,)), dma((len(GROUPS), n)), dma((len(GROUPS), n)), dma((2,)), dma((2,)),
            dma((len(CHUNKS), per, 2)), dma((len(CHUNKS), per, 2)), dma((len(CHUNKS),)), dma((len(CHUNKS),)),
            dma((len(CHUNKS), layers)), dma((len(CHUNKS),)), dma((len(CHUNKS),)), dma((n,)), dma((n,)),
            pltpu.SMEM((1, slots), jnp.int32), dma, dma,
        ]
        scratch += 2 * [pltpu.VMEM((n, size, own_rows, depth // cut), jnp.float32) for _, size, _, cut in GROUPS]
        scratch += [pltpu.VMEM((local, 2, own_rows, chunk), jnp.float32) for chunk in CHUNKS]
        scratch += 2 * [pltpu.VMEM((slots, 2, own_rows, chunk), jnp.float32) for chunk in CHUNKS]
        if tail:
            scratch += 2 * [pltpu.VMEM((2, slots, own_rows, tail), jnp.float32)]
    else:
        kernel = functools.partial(direct_kernel, n, columns, pack)
        scratch += 2 * [pltpu.VMEM((columns, n, own_rows, depth), jnp.float32)] + results + [
            dma((2,)), dma((n,)), dma((n,)), dma((columns, n)), dma((columns, n)), dma((n,)), dma((n,)),
        ]
    out = pl.pallas_call(
        kernel,
        out_shape=(pltpu.VMEM if KEEP and planes else jax.ShapeDtypeStruct)((part_rows, held_rows), jnp.float32),
        in_specs=[
            pl.BlockSpec(memory_space=pltpu.SMEM),
            pl.BlockSpec(memory_space=pl.ANY),
            pl.BlockSpec(memory_space=pl.ANY),
        ],
        out_specs=pl.BlockSpec(memory_space=pltpu.VMEM),
        scratch_shapes=scratch,
        compiler_params=pltpu.CompilerParams(
            collective_id=0, has_side_effects=True, vmem_limit_bytes=60 * 1024 * 1024),
    )(tasks[0], amplitudes, integrals[0, 0])
    return out[None]


def solution(mesh):
    return jax.shard_map(
        functools.partial(body, mesh.shape["pair"], mesh.shape["grp"]),
        mesh=mesh,
        in_specs=(
            P("pair", None, None),
            P("grp", "pair", None, None, None),
            P("grp", "pair", None),
        ),
        out_specs=P("grp", "pair", None),
        check_vma=False,
    )
```

```python
import functools

import jax
import jax.numpy as jnp
from jax import lax
from jax.experimental import pallas as pl
from jax.experimental.pallas import tpu as pltpu
from jax.sharding import PartitionSpec as P

NT = 8
CHUNKS = (384, 512, 640, 768, 768, 640, 384)
GROUPS = ((0, 3, 0, 1), (3, 1, 0, 2), (3, 1, 1, 2))
DUTY = ((), (2, 3), (4, 5, 0), (6, 7, 1))
SHIFT = 1
MESH = pl.DeviceIdType.MESH


def split(x):
    high = x.astype(jnp.bfloat16)
    low = (x - high.astype(jnp.float32)).astype(jnp.bfloat16)
    return jnp.concatenate([high, low], axis=0)


def multiply(rows, operand):
    operand = operand.reshape(-1, operand.shape[-1])
    return lax.dot_general(rows, split(operand), (((1,), (1,)), ((), ())), preferred_element_type=jnp.float32)


def tile_totals(tasks_ref, both, total, n, local, width, part_rows, pack, chosen_slots, more=False):
    piece = part_rows // pack
    tiles, terms = {}, {}
    for slot in chosen_slots:
        code = tasks_ref[0, slot]
        tiles[slot] = jnp.where(code >= 0, lax.div(jnp.maximum(code, 0), local), -1)
        term = both[slot]
        term = term[:width] + term[width:]
        half = term.shape[1] // 2
        terms[slot] = term[:, :half] + term[:, half:]
    packed = {}
    for p in range(n):
        first = p * part_rows
        low = first % width
        value = total[p] if more else jnp.zeros(total.shape[1:], jnp.float32)
        for slot in chosen_slots:
            if (slot, low) not in packed:
                packed[slot, low] = jnp.concatenate(
                    [terms[slot][low + i * piece: low + (i + 1) * piece] for i in range(pack)], axis=1)
            value += jnp.where(tiles[slot] == first // width, packed[slot, low], 0.0)
        total[p] = value


def write_sum(parts, out_ref, pack):
    n = parts.shape[0]
    piece = out_ref.shape[0] // pack
    held_rows = out_ref.shape[1]
    result = parts[0]
    for p in range(1, n):
        result += parts[p]
    for i in range(pack):
        out_ref[i * piece: (i + 1) * piece, :] = result[:, i * held_rows: (i + 1) * held_rows]


def plane_kernel(layers, pack, tasks_ref, amp_ref, int_ref, out_ref, listed, amp, blocks, rows, chosen, both, total,
                 parts, amp_sem, int_sem, list_send, list_recv, near_send, near_recv, tail_send, tail_recv, fetch_send,
                 fetch_recv, own_send, second_send, layer_recv,
                 pick_send, pick_recv, part_send, part_recv, outer_list, outer_send, outer_recv, *buffers):
    n = 8
    me = lax.axis_index("pair")
    grp = lax.axis_index("grp")
    own_rows, pairs, depth = amp_ref.shape
    slots, width, _ = int_ref.shape
    local = pairs // n
    per = local // layers
    shared = sum(CHUNKS)
    tail = depth - shared
    sent, held = buffers[:len(GROUPS)], buffers[len(GROUPS): 2 * len(GROUPS)]
    far = buffers[2 * len(GROUPS): 2 * len(GROUPS) + len(CHUNKS)]
    used = 2 * len(GROUPS) + len(CHUNKS)
    pick_sent, pick_held = buffers[used: used + len(CHUNKS)], buffers[used + len(CHUNKS): used + 2 * len(CHUNKS)]
    tail_sent, tail_held = buffers[-2:] if tail else (None, None)
    starts = [sum(CHUNKS[:q]) for q in range(len(CHUNKS))]
    spans = [pl.ds(part * depth // parts_of, depth // parts_of) for _, _, part, parts_of in GROUPS]

    def bit(value, d):
        return value if not d else 1 - value

    core, x, y = lax.rem(me, 2), lax.rem(me // 2, 2), me // 4
    peer = [bit(y, d // 4) * 4 + bit(x, d // 2 % 2) * 2 + bit(core, d % 2) for d in range(n)]
    near = (2, 4, 3, 5, 1)
    chunks = len(CHUNKS)
    last = chunks - 1
    order = sum(DUTY, ())
    distant = (6, 7)
    inner = (grp >= 1) & (grp <= 2)
    inward = lax.rem(grp, 2) + 1
    outward = (grp - 1) * 3
    second = jnp.where(inner, 3 - outward, 3 - inward)

    def target(d):
        return (peer[d], grp)

    load_amp = pltpu.make_async_copy(amp_ref, amp, amp_sem)
    load_int = pltpu.make_async_copy(int_ref, blocks, int_sem)
    load_amp.start()

    barrier = pltpu.get_barrier_semaphore()
    for d in (6, 7, 2, 3, 4, 5, 1):
        pl.semaphore_signal(barrier, inc=1, device_id=target(d), device_id_type=MESH)

    pl.semaphore_signal(barrier, inc=1, device_id=(me, inward), device_id_type=MESH)
    pl.semaphore_signal(barrier, inc=1, device_id=(me, second), device_id_type=MESH)

    @pl.when(inner)
    def _():
        pl.semaphore_signal(barrier, inc=1, device_id=(me, outward), device_id_type=MESH)

    pl.semaphore_wait(barrier, n + 1 + jnp.where(inner, 1, 0))

    def list_copy(d, receive=False):
        return pltpu.make_async_remote_copy(
            src_ref=tasks_ref, dst_ref=listed.at[peer[d] if receive else me], send_sem=list_send.at[d],
            recv_sem=list_recv.at[d], device_id=target(d), device_id_type=MESH)

    def near_copy(group, d, receive=False):
        return pltpu.make_async_remote_copy(
            src_ref=sent[group].at[peer[d]], dst_ref=held[group].at[peer[d] if receive else me],
            send_sem=near_send.at[group, d], recv_sem=near_recv.at[group, d], device_id=target(d),
            device_id_type=MESH)

    def tail_copy(f):
        return pltpu.make_async_remote_copy(
            src_ref=tail_sent.at[f], dst_ref=tail_held.at[f], send_sem=tail_send.at[f], recv_sem=tail_recv.at[f],
            device_id=target(distant[f]), device_id_type=MESH)

    def fetch_copy(q, j, f, column=None, place=None):
        column = grp * per + j if column is None else column
        place = column if place is None else place
        return pltpu.make_async_remote_copy(
            src_ref=amp_ref.at[:, peer[distant[f]] * local + column, pl.ds(starts[q], CHUNKS[q])],
            dst_ref=far[q].at[place, f],
            send_sem=fetch_send.at[q, j, f], recv_sem=fetch_recv.at[q, j, f], device_id=target(distant[f]),
            device_id_type=MESH)

    def layer_copy(block, q, send, to):
        if q == last and SHIFT:
            at = far[q].at[pl.ds(order.index(DUTY[block][0]), len(DUTY[block]))]
        else:
            at = far[q].at[pl.ds(block * per, per)]
        return pltpu.make_async_remote_copy(
            src_ref=at, dst_ref=at, send_sem=send.at[q], recv_sem=layer_recv.at[q, block], device_id=(me, to),
            device_id_type=MESH)

    def own_copy(q, block=None):
        return layer_copy(grp if block is None else block, q, own_send, inward)

    def second_copy(q, block=None):
        return layer_copy(grp if block is None else block, q, second_send, second)

    def shifted(act):
        for g, columns in enumerate(DUTY):
            if columns:
                @pl.when(grp == g)
                def _():
                    act(g, [(j, f, e, order.index(e)) for j, e in enumerate(columns) for f in range(len(distant))])

    def pick_copy(q, to):
        return pltpu.make_async_remote_copy(
            src_ref=pick_sent[q], dst_ref=pick_held[q], send_sem=pick_send.at[q], recv_sem=pick_recv.at[q],
            device_id=(me, to), device_id_type=MESH)

    outer_copy = pltpu.make_async_remote_copy(
        src_ref=tasks_ref, dst_ref=outer_list, send_sem=outer_send, recv_sem=outer_recv, device_id=(me, inward),
        device_id_type=MESH)

    def part_copy(d, receive=False):
        return pltpu.make_async_remote_copy(
            src_ref=total.at[peer[d]], dst_ref=parts.at[peer[d] if receive else me], send_sem=part_send.at[d],
            recv_sem=part_recv.at[d], device_id=target(d), device_id_type=MESH)

    fetches = [(j, f) for j in range(per) for f in range(len(distant))]
    for j, f in fetches:
        fetch_copy(0, j, f).start()
    for d in range(1, n):
        list_copy(d).start()

    @pl.when(jnp.logical_not(inner))
    def _():
        outer_copy.start()

    for q in range(1, chunks - SHIFT):
        for j, f in fetches:
            fetch_copy(q, j, f).start()
    if SHIFT:
        shifted(lambda g, items: [fetch_copy(last, *item).start() for item in items])

    for d in distant:
        for group in range(len(GROUPS)):
            held[group][peer[d]] = jnp.zeros_like(held[group][peer[d]])
    chosen[...] = jnp.zeros_like(chosen)
    both[...] = jnp.zeros_like(both)
    def local_pair(code):
        return lax.rem(jnp.maximum(code, 0), local)

    def place(q, code):
        e = local_pair(code)
        if q == last and SHIFT:
            return sum(jnp.where(e == c, at, 0) for at, c in enumerate(order))
        return e

    def column(p, slot, code):
        return p * local + local_pair(code)

    pieces = [(group, d) for group in range(len(GROUPS)) for d in near + (0,)]

    def send_near(count):
        for group, d in pieces[:count]:
            for k in range(GROUPS[group][1]):
                slot = GROUPS[group][0] + k
                code = listed[peer[d], 0, slot] if d else tasks_ref[0, slot]
                at = column(peer[d], slot, code)
                to = sent[group] if d else held[group]
                for row in range(own_rows):
                    to[peer[d], k, pl.ds(row, 1), :] = amp[row, pl.ds(at, 1), spans[group]]
            if d:
                near_copy(group, d).start()
        del pieces[:count]

    def send_tail():
        for f, d in enumerate(distant):
            for slot in range(slots):
                at = column(peer[d], slot, listed[peer[d], 0, slot])
                for row in range(own_rows):
                    tail_sent[f, slot, pl.ds(row, 1), :] = amp[row, pl.ds(at, 1), pl.ds(shared, tail)]
            tail_copy(f).start()


    def fetched(q):
        if q == last and SHIFT:
            def act(g, items):
                for item in items:
                    fetch_copy(q, *item).wait_recv()
                if g == layers - 1:
                    second_copy(q, g).start()
                own_copy(q, g).start()

            shifted(act)
            return

        for j, f in fetches:
            fetch_copy(q, j, f).wait_recv()

        @pl.when(jnp.logical_not(inner))
        def _():
            second_copy(q).start()

        own_copy(q).start()

    def select(q):
        @pl.when(inner)
        def _():
            if q == last and SHIFT:
                for g in (1, 2):
                    @pl.when(grp == g)
                    def _():
                        for block in (3 - g, 3):
                            layer_copy(block, q, own_send, inward).wait_recv()
            else:
                for block in (outward, inward, second):
                    layer_copy(block, q, own_send, inward).wait_recv()
            for slot in range(slots):
                pick_sent[q][slot] = far[q][place(q, outer_list[0, slot])]
            pick_copy(q, outward).start()

    def near_part(group):
        for d in near:
            near_copy(group, d, True).wait_recv()
        for k in range(GROUPS[group][1]):
            slot = GROUPS[group][0] + k
            both[slot] += multiply(rows[slot, :, spans[group]], held[group][:, k])

    def far_part(q):
        @pl.when(inner)
        def _():
            for slot in range(slots):
                for f, d in enumerate(distant):
                    chosen[slot, peer[d], :, :CHUNKS[q]] = far[q][place(q, tasks_ref[0, slot]), f]

        @pl.when(jnp.logical_not(inner))
        def _():
            pick_copy(q, inward).wait_recv()
            for slot in range(slots):
                for f, d in enumerate(distant):
                    chosen[slot, peer[d], :, :CHUNKS[q]] = pick_held[q][slot, f]

        for slot in range(slots):
            both[slot] += multiply(rows[slot, :, pl.ds(starts[q], CHUNKS[q])], chosen[slot, :, :, :CHUNKS[q]])

    def tail_part():
        for f in range(len(distant)):
            tail_copy(f).wait_recv()
        for slot in range(slots):
            for f, d in enumerate(distant):
                chosen[slot, peer[d], :, :tail] = tail_held[f, slot]
            both[slot] += multiply(rows[slot, :, pl.ds(shared, tail)], chosen[slot, :, :, :tail])

    @pl.when(inner)
    def _():
        outer_copy.wait_recv()

    fetched(0)
    load_amp.wait()
    for d in range(1, n):
        list_copy(d, True).wait_recv()
    send_near(2)
    fetched(1)
    send_near(2)
    select(0)
    load_int.start()
    for q in range(2, chunks):
        send_near(2)
        fetched(q)
        if q == 2 and tail:
            send_tail()
        if q < last:
            select(q - 1)
    send_near(len(pieces))
    load_int.wait()

    @pl.loop(0, slots)
    def _(slot):
        rows[slot] = split(blocks[slot])

    for q in range(max(1, last - 1), chunks):
        select(q)
    for d in range(1, n):
        list_copy(d).wait_send()
    for q in range(chunks - SHIFT):
        for j, f in fetches:
            fetch_copy(q, j, f).wait_send()
        own_copy(q).wait_send()
    if SHIFT:
        shifted(lambda g, items: [fetch_copy(last, *item).wait_send() for item in items]
                + [own_copy(last, g).wait_send()])
    near_part(0)
    for q in range(chunks):
        far_part(q)
    if tail:
        tail_part()
    totals = functools.partial(tile_totals, tasks_ref, both, total, n, local, width, out_ref.shape[0], pack)
    last_slot = GROUPS[-1][0]
    totals(range(last_slot))
    for d in near:
        near_copy(0, d).wait_send()
    for group in range(1, len(GROUPS)):
        near_part(group)
    totals(range(last_slot, slots), True)
    for d in (6, 7, 2, 4, 3, 5, 1):
        part_copy(d).start()
    parts[me] = total[me]
    for group in range(1, len(GROUPS)):
        for d in near:
            near_copy(group, d).wait_send()
    if tail:
        for f in range(len(distant)):
            tail_copy(f).wait_send()

    @pl.when(inner)
    def _():
        for q in range(chunks):
            pick_copy(q, outward).wait_send()

    @pl.when(jnp.logical_not(inner))
    def _():
        outer_copy.wait_send()
        for q in range(chunks - SHIFT):
            second_copy(q).wait_send()

    if SHIFT:
        @pl.when(grp == layers - 1)
        def _():
            second_copy(last, layers - 1).wait_send()

    for d in (1, 2, 4, 3, 5, 6, 7):
        part_copy(d).wait_send()
    for d in (1, 2, 4, 3, 5, 6, 7):
        part_copy(d, True).wait_recv()
    write_sum(parts, out_ref, pack)


def direct_kernel(n, columns, pack, tasks_ref, amp_ref, int_ref, out_ref, listed, amp, blocks, rows, sent, held, both,
                  total, parts, local_sem, list_send, list_recv, send_sem, recv_sem, part_send, part_recv):
    me = lax.axis_index("pair")
    grp = lax.axis_index("grp")
    own_rows, pairs, depth = amp_ref.shape
    slots, width, _ = int_ref.shape
    local = pairs // n
    lists = columns < local

    load_amp = pltpu.make_async_copy(amp_ref, amp, local_sem.at[0])
    load_int = pltpu.make_async_copy(int_ref, blocks, local_sem.at[1])
    load_amp.start()
    load_int.start()

    def other(d):
        return lax.rem(me + d, n)

    def target(p):
        return (p, grp)

    barrier = pltpu.get_barrier_semaphore()

    @pl.loop(1, n)
    def _(d):
        pl.semaphore_signal(barrier, inc=1, device_id=target(other(d)), device_id_type=MESH)

    pl.semaphore_wait(barrier, n - 1)

    def list_copy(frm, to):
        return pltpu.make_async_remote_copy(
            src_ref=tasks_ref, dst_ref=listed.at[frm], send_sem=list_send.at[to], recv_sem=list_recv.at[frm],
            device_id=target(to), device_id_type=MESH)

    def column_copy(c, frm, to):
        return pltpu.make_async_remote_copy(
            src_ref=sent.at[c, to], dst_ref=held.at[c, frm], send_sem=send_sem.at[c, to],
            recv_sem=recv_sem.at[c, frm], device_id=target(to), device_id_type=MESH)

    def part_copy(frm, to):
        return pltpu.make_async_remote_copy(
            src_ref=total.at[to], dst_ref=parts.at[frm], send_sem=part_send.at[to],
            recv_sem=part_recv.at[frm], device_id=target(to), device_id_type=MESH)

    if lists:
        @pl.loop(1, n)
        def _(d):
            list_copy(me, other(d)).start()

    load_amp.wait()

    if lists:
        @pl.loop(1, n)
        def _(d):
            list_copy(other(d), other(d)).wait_recv()

    def column(p, c, codes):
        if lists:
            return p * local + lax.rem(jnp.maximum(codes(c), 0), local)
        return p * local + c

    for c in range(columns):
        @pl.loop(1, n)
        def _(d):
            p = other(d)
            at = column(p, c, lambda k: listed[p, 0, k])
            for row in range(own_rows):
                sent[c, p, pl.ds(row, 1), :] = amp[row, pl.ds(at, 1), :]

            @pl.when(d > 1)
            def _():
                column_copy(c, me, other(d - 1)).start()

        at = column(me, c, lambda k: tasks_ref[0, k])
        for row in range(own_rows):
            held[c, me, pl.ds(row, 1), :] = amp[row, pl.ds(at, 1), :]
        column_copy(c, me, other(n - 1)).start()

    load_int.wait()

    @pl.loop(0, slots)
    def _(slot):
        rows[slot] = split(blocks[slot])

    def arrive(c):
        @pl.loop(1, n)
        def _(d):
            column_copy(c, other(d), other(d)).wait_recv()

    if lists:
        for slot in range(slots):
            arrive(slot)
            both[slot] = multiply(rows[slot], held[slot])
    else:
        for c in range(columns):
            arrive(c)

        @pl.loop(0, slots)
        def _(slot):
            both[slot] = multiply(rows[slot], held[lax.rem(jnp.maximum(tasks_ref[0, slot], 0), local)])

    tile_totals(tasks_ref, both, total, n, local, width, out_ref.shape[0], pack, range(slots))

    @pl.loop(1, n)
    def _(d):
        part_copy(me, other(d)).start()

    parts[me] = total[me]

    @pl.loop(1, n)
    def _(d):
        part_copy(other(d), other(d)).wait_recv()

    write_sum(parts, out_ref, pack)

    @pl.loop(1, n)
    def _(d):
        part_copy(me, other(d)).wait_send()
        if lists:
            list_copy(me, other(d)).wait_send()
        for c in range(columns):
            column_copy(c, me, other(d)).wait_send()


def body(n, layers, amplitudes, integrals, tasks):
    own_rows, pairs, depth = amplitudes.shape
    slots, width = integrals.shape[2:4]
    local = pairs // n
    columns = min(local, slots)
    part_rows = NT * width // n
    held_rows = n * own_rows
    pack = max(1, 128 // held_rows)
    tail = depth - sum(CHUNKS)
    planes = n == 8 and layers == 4 and local == 8 and slots == 4 and tail >= 0
    dma = pltpu.SemaphoreType.DMA
    scratch = [
        pltpu.SMEM((n, 1, slots), jnp.int32),
        pltpu.VMEM(amplitudes.shape, jnp.float32),
        pltpu.VMEM((slots, width, depth), jnp.float32),
        pltpu.VMEM((slots, 2 * width, depth), jnp.bfloat16),
    ]
    results = [
        pltpu.VMEM((slots, 2 * width, 2 * held_rows), jnp.float32),
        pltpu.VMEM((n, part_rows // pack, held_rows * pack), jnp.float32),
        pltpu.VMEM((n, part_rows // pack, held_rows * pack), jnp.float32),
    ]
    if planes:
        kernel = functools.partial(plane_kernel, layers, pack)
        scratch += [pltpu.VMEM((slots, n, own_rows, max(CHUNKS + (tail,))), jnp.float32)] + results + [
            dma, dma, dma((n,)), dma((n,)), dma((len(GROUPS), n)), dma((len(GROUPS), n)), dma((2,)), dma((2,)),
            dma((len(CHUNKS), 3, 2)), dma((len(CHUNKS), 3, 2)), dma((len(CHUNKS),)), dma((len(CHUNKS),)),
            dma((len(CHUNKS), layers)), dma((len(CHUNKS),)), dma((len(CHUNKS),)), dma((n,)), dma((n,)),
            pltpu.SMEM((1, slots), jnp.int32), dma, dma,
        ]
        scratch += 2 * [pltpu.VMEM((n, size, own_rows, depth // cut), jnp.float32) for _, size, _, cut in GROUPS]
        scratch += [pltpu.VMEM((local, 2, own_rows, chunk), jnp.float32) for chunk in CHUNKS]
        scratch += 2 * [pltpu.VMEM((slots, 2, own_rows, chunk), jnp.float32) for chunk in CHUNKS]
        if tail:
            scratch += 2 * [pltpu.VMEM((2, slots, own_rows, tail), jnp.float32)]
    else:
        kernel = functools.partial(direct_kernel, n, columns, pack)
        scratch += 2 * [pltpu.VMEM((columns, n, own_rows, depth), jnp.float32)] + results + [
            dma((2,)), dma((n,)), dma((n,)), dma((columns, n)), dma((columns, n)), dma((n,)), dma((n,)),
        ]
    out = pl.pallas_call(
        kernel,
        out_shape=(pltpu.VMEM if planes else jax.ShapeDtypeStruct)((part_rows, held_rows), jnp.float32),
        in_specs=[
            pl.BlockSpec(memory_space=pltpu.SMEM),
            pl.BlockSpec(memory_space=pl.ANY),
            pl.BlockSpec(memory_space=pl.ANY),
        ],
        out_specs=pl.BlockSpec(memory_space=pltpu.VMEM),
        scratch_shapes=scratch,
        compiler_params=pltpu.CompilerParams(
            collective_id=0, has_side_effects=True, vmem_limit_bytes=60 * 1024 * 1024),
    )(tasks[0], amplitudes, integrals[0, 0])
    return out[None]


def solution(mesh):
    return jax.shard_map(
        functools.partial(body, mesh.shape["pair"], mesh.shape["grp"]),
        mesh=mesh,
        in_specs=(
            P("pair", None, None),
            P("grp", "pair", None, None, None),
            P("grp", "pair", None),
        ),
        out_specs=P("grp", "pair", None),
        check_vma=False,
    )
```

```python
import functools

import jax
import jax.numpy as jnp
from jax import lax
from jax.experimental import pallas as pl
from jax.experimental.pallas import tpu as pltpu
from jax.sharding import PartitionSpec as P

NT = 8
CHUNKS = (384, 512, 640, 768, 768, 640, 384)
GROUPS = ((0, 4, 0, 3584), (0, 4, 3584, 512))
EARLY = 5
DUTY = ((), (2, 3), (4, 5, 0), (6, 7, 1))
SHIFT = 1
STEP = 1
MESH = pl.DeviceIdType.MESH


def split(x):
    high = x.astype(jnp.bfloat16)
    low = (x - high.astype(jnp.float32)).astype(jnp.bfloat16)
    return jnp.concatenate([high, low], axis=0)


def multiply(rows, operand):
    operand = operand.reshape(-1, operand.shape[-1])
    return lax.dot_general(rows, split(operand), (((1,), (1,)), ((), ())), preferred_element_type=jnp.float32)


def tile_totals(tasks_ref, both, total, n, local, width, part_rows, pack, chosen_slots, more=False):
    piece = part_rows // pack
    tiles, terms = {}, {}
    for slot in chosen_slots:
        code = tasks_ref[0, slot]
        tiles[slot] = jnp.where(code >= 0, lax.div(jnp.maximum(code, 0), local), -1)
        term = both[slot]
        term = term[:width] + term[width:]
        half = term.shape[1] // 2
        terms[slot] = term[:, :half] + term[:, half:]
    packed = {}
    for p in range(n):
        first = p * part_rows
        low = first % width
        value = total[p] if more else jnp.zeros(total.shape[1:], jnp.float32)
        for slot in chosen_slots:
            if (slot, low) not in packed:
                packed[slot, low] = jnp.concatenate(
                    [terms[slot][low + i * piece: low + (i + 1) * piece] for i in range(pack)], axis=1)
            value += jnp.where(tiles[slot] == first // width, packed[slot, low], 0.0)
        total[p] = value


def write_sum(parts, out_ref, pack):
    n = parts.shape[0]
    piece = out_ref.shape[0] // pack
    held_rows = out_ref.shape[1]
    result = parts[0]
    for p in range(1, n):
        result += parts[p]
    for i in range(pack):
        out_ref[i * piece: (i + 1) * piece, :] = result[:, i * held_rows: (i + 1) * held_rows]


def plane_kernel(layers, pack, tasks_ref, amp_ref, int_ref, out_ref, listed, amp, blocks, rows, chosen, both, total,
                 parts, amp_sem, int_sem, list_send, list_recv, near_send, near_recv, tail_send, tail_recv, fetch_send,
                 fetch_recv, own_send, second_send, layer_recv,
                 pick_send, pick_recv, part_send, part_recv, outer_list, outer_send, outer_recv, *buffers):
    n = 8
    me = lax.axis_index("pair")
    grp = lax.axis_index("grp")
    own_rows, pairs, depth = amp_ref.shape
    slots, width, _ = int_ref.shape
    local = pairs // n
    per = local // layers
    shared = sum(CHUNKS)
    tail = depth - shared
    sent, held = buffers[:len(GROUPS)], buffers[len(GROUPS): 2 * len(GROUPS)]
    far = buffers[2 * len(GROUPS): 2 * len(GROUPS) + len(CHUNKS)]
    used = 2 * len(GROUPS) + len(CHUNKS)
    pick_sent, pick_held = buffers[used: used + len(CHUNKS)], buffers[used + len(CHUNKS): used + 2 * len(CHUNKS)]
    tail_sent, tail_held = buffers[-2:] if tail else (None, None)
    starts = [sum(CHUNKS[:q]) for q in range(len(CHUNKS))]
    spans = [pl.ds(start, size) for _, _, start, size in GROUPS]

    def bit(value, d):
        return value if not d else 1 - value

    core, x, y = lax.rem(me, 2), lax.rem(me // 2, 2), me // 4
    peer = [bit(y, d // 4) * 4 + bit(x, d // 2 % 2) * 2 + bit(core, d % 2) for d in range(n)]
    near = (2, 4, 3, 5, 1)
    chunks = len(CHUNKS)
    last = chunks - 1
    order = sum(DUTY, ())
    distant = (6, 7)
    inner = (grp >= 1) & (grp <= 2)
    inward = lax.rem(grp, 2) + 1
    outward = (grp - 1) * 3
    second = jnp.where(inner, 3 - outward, 3 - inward)

    def target(d):
        return (peer[d], grp)

    load_amp = pltpu.make_async_copy(amp_ref, amp, amp_sem)
    load_int = pltpu.make_async_copy(int_ref, blocks, int_sem)
    load_amp.start()

    barrier = pltpu.get_barrier_semaphore()
    for d in (6, 7, 2, 3, 4, 5, 1):
        pl.semaphore_signal(barrier, inc=1, device_id=target(d), device_id_type=MESH)

    pl.semaphore_signal(barrier, inc=1, device_id=(me, inward), device_id_type=MESH)
    pl.semaphore_signal(barrier, inc=1, device_id=(me, second), device_id_type=MESH)

    @pl.when(inner)
    def _():
        pl.semaphore_signal(barrier, inc=1, device_id=(me, outward), device_id_type=MESH)

    pl.semaphore_wait(barrier, n + 1 + jnp.where(inner, 1, 0))

    def list_copy(d, receive=False):
        return pltpu.make_async_remote_copy(
            src_ref=tasks_ref, dst_ref=listed.at[peer[d] if receive else me], send_sem=list_send.at[d],
            recv_sem=list_recv.at[d], device_id=target(d), device_id_type=MESH)

    def near_copy(group, d, receive=False):
        return pltpu.make_async_remote_copy(
            src_ref=sent[group].at[peer[d]], dst_ref=held[group].at[peer[d] if receive else me],
            send_sem=near_send.at[group, d], recv_sem=near_recv.at[group, d], device_id=target(d),
            device_id_type=MESH)

    def tail_copy(f):
        return pltpu.make_async_remote_copy(
            src_ref=tail_sent.at[f], dst_ref=tail_held.at[f], send_sem=tail_send.at[f], recv_sem=tail_recv.at[f],
            device_id=target(distant[f]), device_id_type=MESH)

    def fetch_copy(q, j, f, column=None, place=None):
        column = grp * per + j if column is None else column
        place = column if place is None else place
        return pltpu.make_async_remote_copy(
            src_ref=amp_ref.at[:, peer[distant[f]] * local + column, pl.ds(starts[q], CHUNKS[q])],
            dst_ref=far[q].at[place, f],
            send_sem=fetch_send.at[q, j, f], recv_sem=fetch_recv.at[q, j, f], device_id=target(distant[f]),
            device_id_type=MESH)

    def layer_copy(block, q, send, to):
        if q == last and SHIFT:
            at = far[q].at[pl.ds(order.index(DUTY[block][0]), len(DUTY[block]))]
        else:
            at = far[q].at[pl.ds(block * per, per)]
        return pltpu.make_async_remote_copy(
            src_ref=at, dst_ref=at, send_sem=send.at[q], recv_sem=layer_recv.at[q, block], device_id=(me, to),
            device_id_type=MESH)

    def own_copy(q, block=None):
        return layer_copy(grp if block is None else block, q, own_send, inward)

    def second_copy(q, block=None):
        return layer_copy(grp if block is None else block, q, second_send, second)

    def shifted(act):
        for g, columns in enumerate(DUTY):
            if columns:
                @pl.when(grp == g)
                def _():
                    act(g, [(j, f, e, order.index(e)) for j, e in enumerate(columns) for f in range(len(distant))])

    def pick_copy(q, to):
        return pltpu.make_async_remote_copy(
            src_ref=pick_sent[q], dst_ref=pick_held[q], send_sem=pick_send.at[q], recv_sem=pick_recv.at[q],
            device_id=(me, to), device_id_type=MESH)

    outer_copy = pltpu.make_async_remote_copy(
        src_ref=tasks_ref, dst_ref=outer_list, send_sem=outer_send, recv_sem=outer_recv, device_id=(me, inward),
        device_id_type=MESH)

    def part_copy(d, receive=False):
        return pltpu.make_async_remote_copy(
            src_ref=total.at[peer[d]], dst_ref=parts.at[peer[d] if receive else me], send_sem=part_send.at[d],
            recv_sem=part_recv.at[d], device_id=target(d), device_id_type=MESH)

    fetches = [(j, f) for j in range(per) for f in range(len(distant))]
    for j, f in fetches:
        fetch_copy(0, j, f).start()
    for d in range(1, n):
        list_copy(d).start()

    @pl.when(jnp.logical_not(inner))
    def _():
        outer_copy.start()

    for q in range(1, chunks - SHIFT):
        for j, f in fetches:
            fetch_copy(q, j, f).start()
    if SHIFT:
        shifted(lambda g, items: [fetch_copy(last, *item).start() for item in items])

    for d in distant:
        for group in range(len(GROUPS)):
            held[group][peer[d]] = jnp.zeros_like(held[group][peer[d]])
    chosen[...] = jnp.zeros_like(chosen)
    both[...] = jnp.zeros_like(both)
    def local_pair(code):
        return lax.rem(jnp.maximum(code, 0), local)

    def place(q, code):
        e = local_pair(code)
        if q == last and SHIFT:
            return sum(jnp.where(e == c, at, 0) for at, c in enumerate(order))
        return e

    def column(p, slot, code):
        return p * local + local_pair(code)

    pieces = [(group, d) for group in range(len(GROUPS)) for d in near + (0,)]

    def send_near(count):
        for group, d in pieces[:count]:
            for k in range(GROUPS[group][1]):
                slot = GROUPS[group][0] + k
                code = listed[peer[d], 0, slot] if d else tasks_ref[0, slot]
                at = column(peer[d], slot, code)
                to = sent[group] if d else held[group]
                for row in range(own_rows):
                    to[peer[d], k, pl.ds(row, 1), :] = amp[row, pl.ds(at, 1), spans[group]]
            if d:
                near_copy(group, d).start()
        del pieces[:count]

    def send_tail():
        for f, d in enumerate(distant):
            for slot in range(slots):
                at = column(peer[d], slot, listed[peer[d], 0, slot])
                for row in range(own_rows):
                    tail_sent[f, slot, pl.ds(row, 1), :] = amp[row, pl.ds(at, 1), pl.ds(shared, tail)]
            tail_copy(f).start()


    def fetched(q):
        if q == last and SHIFT:
            def act(g, items):
                for item in items:
                    fetch_copy(q, *item).wait_recv()
                if g == layers - 1:
                    second_copy(q, g).start()
                own_copy(q, g).start()

            shifted(act)
            return

        for j, f in fetches:
            fetch_copy(q, j, f).wait_recv()

        @pl.when(jnp.logical_not(inner))
        def _():
            second_copy(q).start()

        own_copy(q).start()

    def select(q):
        @pl.when(inner)
        def _():
            if q == last and SHIFT:
                for g in (1, 2):
                    @pl.when(grp == g)
                    def _():
                        for block in (3 - g, 3):
                            layer_copy(block, q, own_send, inward).wait_recv()
            else:
                for block in (outward, inward, second):
                    layer_copy(block, q, own_send, inward).wait_recv()
            for slot in range(slots):
                pick_sent[q][slot] = far[q][place(q, outer_list[0, slot])]
            pick_copy(q, outward).start()

    def near_part(group):
        for d in near:
            near_copy(group, d, True).wait_recv()
        for k in range(GROUPS[group][1]):
            slot = GROUPS[group][0] + k
            both[slot] += multiply(rows[slot, :, spans[group]], held[group][:, k])

    def far_part(q):
        @pl.when(inner)
        def _():
            for slot in range(slots):
                for f, d in enumerate(distant):
                    chosen[slot, peer[d], :, :CHUNKS[q]] = far[q][place(q, tasks_ref[0, slot]), f]

        @pl.when(jnp.logical_not(inner))
        def _():
            pick_copy(q, inward).wait_recv()
            for slot in range(slots):
                for f, d in enumerate(distant):
                    chosen[slot, peer[d], :, :CHUNKS[q]] = pick_held[q][slot, f]

        for slot in range(slots):
            both[slot] += multiply(rows[slot, :, pl.ds(starts[q], CHUNKS[q])], chosen[slot, :, :, :CHUNKS[q]])

    def tail_part():
        for f in range(len(distant)):
            tail_copy(f).wait_recv()
        for slot in range(slots):
            for f, d in enumerate(distant):
                chosen[slot, peer[d], :, :tail] = tail_held[f, slot]
            both[slot] += multiply(rows[slot, :, pl.ds(shared, tail)], chosen[slot, :, :, :tail])

    @pl.when(inner)
    def _():
        outer_copy.wait_recv()

    fetched(0)
    load_amp.wait()
    for d in range(1, n):
        list_copy(d, True).wait_recv()
    send_near(STEP)
    fetched(1)
    send_near(STEP)
    select(0)
    load_int.start()
    for q in range(2, chunks):
        send_near(2)
        fetched(q)
        if q == 2 and tail:
            send_tail()
        if q < last:
            select(q - 1)
    send_near(len(pieces))
    load_int.wait()

    @pl.loop(0, slots)
    def _(slot):
        rows[slot] = split(blocks[slot])

    for q in range(max(1, last - 1), chunks):
        select(q)
    for d in range(1, n):
        list_copy(d).wait_send()
    for q in range(chunks - SHIFT):
        for j, f in fetches:
            fetch_copy(q, j, f).wait_send()
        own_copy(q).wait_send()
    if SHIFT:
        shifted(lambda g, items: [fetch_copy(last, *item).wait_send() for item in items]
                + [own_copy(last, g).wait_send()])
    for q in range(EARLY):
        far_part(q)
    near_part(0)
    for q in range(EARLY, chunks):
        far_part(q)
    if tail:
        tail_part()
    totals = functools.partial(tile_totals, tasks_ref, both, total, n, local, width, out_ref.shape[0], pack)
    last_slot = GROUPS[-1][0]
    totals(range(last_slot))
    for d in near:
        near_copy(0, d).wait_send()
    for group in range(1, len(GROUPS)):
        near_part(group)
    totals(range(last_slot, slots), True)
    for d in (6, 7, 2, 4, 3, 5, 1):
        part_copy(d).start()
    parts[me] = total[me]
    for group in range(1, len(GROUPS)):
        for d in near:
            near_copy(group, d).wait_send()
    if tail:
        for f in range(len(distant)):
            tail_copy(f).wait_send()

    @pl.when(inner)
    def _():
        for q in range(chunks):
            pick_copy(q, outward).wait_send()

    @pl.when(jnp.logical_not(inner))
    def _():
        outer_copy.wait_send()
        for q in range(chunks - SHIFT):
            second_copy(q).wait_send()

    if SHIFT:
        @pl.when(grp == layers - 1)
        def _():
            second_copy(last, layers - 1).wait_send()

    for d in (1, 2, 4, 3, 5, 6, 7):
        part_copy(d).wait_send()
    for d in (1, 2, 4, 3, 5, 6, 7):
        part_copy(d, True).wait_recv()
    write_sum(parts, out_ref, pack)


def direct_kernel(n, columns, pack, tasks_ref, amp_ref, int_ref, out_ref, listed, amp, blocks, rows, sent, held, both,
                  total, parts, local_sem, list_send, list_recv, send_sem, recv_sem, part_send, part_recv):
    me = lax.axis_index("pair")
    grp = lax.axis_index("grp")
    own_rows, pairs, depth = amp_ref.shape
    slots, width, _ = int_ref.shape
    local = pairs // n
    lists = columns < local

    load_amp = pltpu.make_async_copy(amp_ref, amp, local_sem.at[0])
    load_int = pltpu.make_async_copy(int_ref, blocks, local_sem.at[1])
    load_amp.start()
    load_int.start()

    def other(d):
        return lax.rem(me + d, n)

    def target(p):
        return (p, grp)

    barrier = pltpu.get_barrier_semaphore()

    @pl.loop(1, n)
    def _(d):
        pl.semaphore_signal(barrier, inc=1, device_id=target(other(d)), device_id_type=MESH)

    pl.semaphore_wait(barrier, n - 1)

    def list_copy(frm, to):
        return pltpu.make_async_remote_copy(
            src_ref=tasks_ref, dst_ref=listed.at[frm], send_sem=list_send.at[to], recv_sem=list_recv.at[frm],
            device_id=target(to), device_id_type=MESH)

    def column_copy(c, frm, to):
        return pltpu.make_async_remote_copy(
            src_ref=sent.at[c, to], dst_ref=held.at[c, frm], send_sem=send_sem.at[c, to],
            recv_sem=recv_sem.at[c, frm], device_id=target(to), device_id_type=MESH)

    def part_copy(frm, to):
        return pltpu.make_async_remote_copy(
            src_ref=total.at[to], dst_ref=parts.at[frm], send_sem=part_send.at[to],
            recv_sem=part_recv.at[frm], device_id=target(to), device_id_type=MESH)

    if lists:
        @pl.loop(1, n)
        def _(d):
            list_copy(me, other(d)).start()

    load_amp.wait()

    if lists:
        @pl.loop(1, n)
        def _(d):
            list_copy(other(d), other(d)).wait_recv()

    def column(p, c, codes):
        if lists:
            return p * local + lax.rem(jnp.maximum(codes(c), 0), local)
        return p * local + c

    for c in range(columns):
        @pl.loop(1, n)
        def _(d):
            p = other(d)
            at = column(p, c, lambda k: listed[p, 0, k])
            for row in range(own_rows):
                sent[c, p, pl.ds(row, 1), :] = amp[row, pl.ds(at, 1), :]

            @pl.when(d > 1)
            def _():
                column_copy(c, me, other(d - 1)).start()

        at = column(me, c, lambda k: tasks_ref[0, k])
        for row in range(own_rows):
            held[c, me, pl.ds(row, 1), :] = amp[row, pl.ds(at, 1), :]
        column_copy(c, me, other(n - 1)).start()

    load_int.wait()

    @pl.loop(0, slots)
    def _(slot):
        rows[slot] = split(blocks[slot])

    def arrive(c):
        @pl.loop(1, n)
        def _(d):
            column_copy(c, other(d), other(d)).wait_recv()

    if lists:
        for slot in range(slots):
            arrive(slot)
            both[slot] = multiply(rows[slot], held[slot])
    else:
        for c in range(columns):
            arrive(c)

        @pl.loop(0, slots)
        def _(slot):
            both[slot] = multiply(rows[slot], held[lax.rem(jnp.maximum(tasks_ref[0, slot], 0), local)])

    tile_totals(tasks_ref, both, total, n, local, width, out_ref.shape[0], pack, range(slots))

    @pl.loop(1, n)
    def _(d):
        part_copy(me, other(d)).start()

    parts[me] = total[me]

    @pl.loop(1, n)
    def _(d):
        part_copy(other(d), other(d)).wait_recv()

    write_sum(parts, out_ref, pack)

    @pl.loop(1, n)
    def _(d):
        part_copy(me, other(d)).wait_send()
        if lists:
            list_copy(me, other(d)).wait_send()
        for c in range(columns):
            column_copy(c, me, other(d)).wait_send()


def body(n, layers, amplitudes, integrals, tasks):
    own_rows, pairs, depth = amplitudes.shape
    slots, width = integrals.shape[2:4]
    local = pairs // n
    columns = min(local, slots)
    part_rows = NT * width // n
    held_rows = n * own_rows
    pack = max(1, 128 // held_rows)
    tail = depth - sum(CHUNKS)
    planes = n == 8 and layers == 4 and local == 8 and slots == 4 and depth == 4096
    dma = pltpu.SemaphoreType.DMA
    scratch = [
        pltpu.SMEM((n, 1, slots), jnp.int32),
        pltpu.VMEM(amplitudes.shape, jnp.float32),
        pltpu.VMEM((slots, width, depth), jnp.float32),
        pltpu.VMEM((slots, 2 * width, depth), jnp.bfloat16),
    ]
    results = [
        pltpu.VMEM((slots, 2 * width, 2 * held_rows), jnp.float32),
        pltpu.VMEM((n, part_rows // pack, held_rows * pack), jnp.float32),
        pltpu.VMEM((n, part_rows // pack, held_rows * pack), jnp.float32),
    ]
    if planes:
        kernel = functools.partial(plane_kernel, layers, pack)
        scratch += [pltpu.VMEM((slots, n, own_rows, max(CHUNKS + (tail,))), jnp.float32)] + results + [
            dma, dma, dma((n,)), dma((n,)), dma((len(GROUPS), n)), dma((len(GROUPS), n)), dma((2,)), dma((2,)),
            dma((len(CHUNKS), 3, 2)), dma((len(CHUNKS), 3, 2)), dma((len(CHUNKS),)), dma((len(CHUNKS),)),
            dma((len(CHUNKS), layers)), dma((len(CHUNKS),)), dma((len(CHUNKS),)), dma((n,)), dma((n,)),
            pltpu.SMEM((1, slots), jnp.int32), dma, dma,
        ]
        scratch += 2 * [pltpu.VMEM((n, count, own_rows, size), jnp.float32) for _, count, _, size in GROUPS]
        scratch += [pltpu.VMEM((local, 2, own_rows, chunk), jnp.float32) for chunk in CHUNKS]
        scratch += 2 * [pltpu.VMEM((slots, 2, own_rows, chunk), jnp.float32) for chunk in CHUNKS]
        if tail:
            scratch += 2 * [pltpu.VMEM((2, slots, own_rows, tail), jnp.float32)]
    else:
        kernel = functools.partial(direct_kernel, n, columns, pack)
        scratch += 2 * [pltpu.VMEM((columns, n, own_rows, depth), jnp.float32)] + results + [
            dma((2,)), dma((n,)), dma((n,)), dma((columns, n)), dma((columns, n)), dma((n,)), dma((n,)),
        ]
    out = pl.pallas_call(
        kernel,
        out_shape=(pltpu.VMEM if planes else jax.ShapeDtypeStruct)((part_rows, held_rows), jnp.float32),
        in_specs=[
            pl.BlockSpec(memory_space=pltpu.SMEM),
            pl.BlockSpec(memory_space=pl.ANY),
            pl.BlockSpec(memory_space=pl.ANY),
        ],
        out_specs=pl.BlockSpec(memory_space=pltpu.VMEM),
        scratch_shapes=scratch,
        compiler_params=pltpu.CompilerParams(
            collective_id=0, has_side_effects=True, vmem_limit_bytes=60 * 1024 * 1024),
    )(tasks[0], amplitudes, integrals[0, 0])
    return out[None]


def solution(mesh):
    return jax.shard_map(
        functools.partial(body, mesh.shape["pair"], mesh.shape["grp"]),
        mesh=mesh,
        in_specs=(
            P("pair", None, None),
            P("grp", "pair", None, None, None),
            P("grp", "pair", None),
        ),
        out_specs=P("grp", "pair", None),
        check_vma=False,
    )
```

```python
import functools

import jax
import jax.numpy as jnp
from jax import lax
from jax.experimental import pallas as pl
from jax.experimental.pallas import tpu as pltpu
from jax.sharding import PartitionSpec as P

NT = 8
CHUNKS = (384, 512, 640, 768, 768, 640, 384)
FETCHED = ((0,), (1,), (2, 3), (4, 5))
GROUPS = ((0, 4, 0, 3584), (0, 4, 3584, 512))
EARLY = 5
DUTY = ((), (2, 3), (4, 5, 0), (6, 7, 1))
SHIFT = 1
STEP = 1
MESH = pl.DeviceIdType.MESH


def split(x):
    high = x.astype(jnp.bfloat16)
    low = (x - high.astype(jnp.float32)).astype(jnp.bfloat16)
    return jnp.concatenate([high, low], axis=0)


def multiply(rows, operand):
    operand = operand.reshape(-1, operand.shape[-1])
    return lax.dot_general(rows, split(operand), (((1,), (1,)), ((), ())), preferred_element_type=jnp.float32)


def tile_totals(tasks_ref, both, total, n, local, width, part_rows, pack, chosen_slots, more=False):
    piece = part_rows // pack
    tiles, terms = {}, {}
    for slot in chosen_slots:
        code = tasks_ref[0, slot]
        tiles[slot] = jnp.where(code >= 0, lax.div(jnp.maximum(code, 0), local), -1)
        term = both[slot]
        term = term[:width] + term[width:]
        half = term.shape[1] // 2
        terms[slot] = term[:, :half] + term[:, half:]
    packed = {}
    for p in range(n):
        first = p * part_rows
        low = first % width
        value = total[p] if more else jnp.zeros(total.shape[1:], jnp.float32)
        for slot in chosen_slots:
            if (slot, low) not in packed:
                packed[slot, low] = jnp.concatenate(
                    [terms[slot][low + i * piece: low + (i + 1) * piece] for i in range(pack)], axis=1)
            value += jnp.where(tiles[slot] == first // width, packed[slot, low], 0.0)
        total[p] = value


def write_sum(parts, out_ref, pack):
    n = parts.shape[0]
    piece = out_ref.shape[0] // pack
    held_rows = out_ref.shape[1]
    result = parts[0]
    for p in range(1, n):
        result += parts[p]
    for i in range(pack):
        out_ref[i * piece: (i + 1) * piece, :] = result[:, i * held_rows: (i + 1) * held_rows]


def plane_kernel(layers, pack, tasks_ref, amp_ref, int_ref, out_ref, listed, amp, blocks, rows, chosen, both, total,
                 parts, amp_sem, int_sem, list_send, list_recv, near_send, near_recv, tail_send, tail_recv, fetch_send,
                 fetch_recv, own_send, second_send, layer_recv,
                 pick_send, pick_recv, part_send, part_recv, outer_list, outer_send, outer_recv, *buffers):
    n = 8
    me = lax.axis_index("pair")
    grp = lax.axis_index("grp")
    own_rows, pairs, depth = amp_ref.shape
    slots, width, _ = int_ref.shape
    local = pairs // n
    per = local // layers
    shared = sum(CHUNKS)
    tail = depth - shared
    sent, held = buffers[:len(GROUPS)], buffers[len(GROUPS): 2 * len(GROUPS)]
    far = buffers[2 * len(GROUPS): 2 * len(GROUPS) + len(CHUNKS)]
    used = 2 * len(GROUPS) + len(CHUNKS)
    pick_sent, pick_held = buffers[used: used + len(CHUNKS)], buffers[used + len(CHUNKS): used + 2 * len(CHUNKS)]
    tail_sent, tail_held = buffers[-2 - len(FETCHED): -len(FETCHED)] if tail else (None, None)
    starts = [sum(CHUNKS[:q]) for q in range(len(CHUNKS))]
    spans = [pl.ds(start, size) for _, _, start, size in GROUPS]

    def bit(value, d):
        return value if not d else 1 - value

    core, x, y = lax.rem(me, 2), lax.rem(me // 2, 2), me // 4
    peer = [bit(y, d // 4) * 4 + bit(x, d // 2 % 2) * 2 + bit(core, d % 2) for d in range(n)]
    near = (2, 4, 3, 5, 1)
    chunks = len(CHUNKS)
    last = chunks - 1
    order = sum(DUTY, ())
    landing = buffers[len(buffers) - len(FETCHED):]
    home = {q: m for m, held_chunks in enumerate(FETCHED) for q in held_chunks}
    distant = (6, 7)
    inner = (grp >= 1) & (grp <= 2)
    inward = lax.rem(grp, 2) + 1
    outward = (grp - 1) * 3
    second = jnp.where(inner, 3 - outward, 3 - inward)

    def target(d):
        return (peer[d], grp)

    load_amp = pltpu.make_async_copy(amp_ref, amp, amp_sem)
    load_int = pltpu.make_async_copy(int_ref, blocks, int_sem)
    load_amp.start()

    barrier = pltpu.get_barrier_semaphore()
    for d in (6, 7, 2, 3, 4, 5, 1):
        pl.semaphore_signal(barrier, inc=1, device_id=target(d), device_id_type=MESH)

    pl.semaphore_signal(barrier, inc=1, device_id=(me, inward), device_id_type=MESH)
    pl.semaphore_signal(barrier, inc=1, device_id=(me, second), device_id_type=MESH)

    @pl.when(inner)
    def _():
        pl.semaphore_signal(barrier, inc=1, device_id=(me, outward), device_id_type=MESH)

    pl.semaphore_wait(barrier, n + 1 + jnp.where(inner, 1, 0))

    def list_copy(d, receive=False):
        return pltpu.make_async_remote_copy(
            src_ref=tasks_ref, dst_ref=listed.at[peer[d] if receive else me], send_sem=list_send.at[d],
            recv_sem=list_recv.at[d], device_id=target(d), device_id_type=MESH)

    def near_copy(group, d, receive=False):
        return pltpu.make_async_remote_copy(
            src_ref=sent[group].at[peer[d]], dst_ref=held[group].at[peer[d] if receive else me],
            send_sem=near_send.at[group, d], recv_sem=near_recv.at[group, d], device_id=target(d),
            device_id_type=MESH)

    def tail_copy(f):
        return pltpu.make_async_remote_copy(
            src_ref=tail_sent.at[f], dst_ref=tail_held.at[f], send_sem=tail_send.at[f], recv_sem=tail_recv.at[f],
            device_id=target(distant[f]), device_id_type=MESH)

    def fetch_copy(q, j, f, column=None, at=None):
        if column is None:
            m = home[q]
            column, start, size, to = grp * per + j, starts[FETCHED[m][0]], landing[m].shape[-1], landing[m].at[j, f]
        else:
            m, start, size, to = len(FETCHED), starts[q], CHUNKS[q], far[q].at[at, f]
        return pltpu.make_async_remote_copy(
            src_ref=amp_ref.at[:, peer[distant[f]] * local + column, pl.ds(start, size)], dst_ref=to,
            send_sem=fetch_send.at[m, j, f], recv_sem=fetch_recv.at[m, j, f], device_id=target(distant[f]),
            device_id_type=MESH)

    def landed(q):
        return pl.ds(starts[q] - starts[FETCHED[home[q]][0]], CHUNKS[q])

    def layer_copy(block, q, send, to, own=False):
        if q == last and SHIFT:
            at = far[q].at[pl.ds(order.index(DUTY[block][0]), len(DUTY[block]))]
        else:
            at = far[q].at[pl.ds(block * per, per)]
        frm = landing[home[q]].at[:, :, :, landed(q)] if own and q in home else at
        return pltpu.make_async_remote_copy(
            src_ref=frm, dst_ref=at, send_sem=send.at[q], recv_sem=layer_recv.at[q, block], device_id=(me, to),
            device_id_type=MESH)

    def own_copy(q, block=None):
        return layer_copy(grp if block is None else block, q, own_send, inward, True)

    def second_copy(q, block=None):
        return layer_copy(grp if block is None else block, q, second_send, second, True)

    def shifted(act):
        for g, columns in enumerate(DUTY):
            if columns:
                @pl.when(grp == g)
                def _():
                    act(g, [(j, f, e, order.index(e)) for j, e in enumerate(columns) for f in range(len(distant))])

    def pick_copy(q, to):
        return pltpu.make_async_remote_copy(
            src_ref=pick_sent[q], dst_ref=pick_held[q], send_sem=pick_send.at[q], recv_sem=pick_recv.at[q],
            device_id=(me, to), device_id_type=MESH)

    outer_copy = pltpu.make_async_remote_copy(
        src_ref=tasks_ref, dst_ref=outer_list, send_sem=outer_send, recv_sem=outer_recv, device_id=(me, inward),
        device_id_type=MESH)

    def part_copy(d, receive=False):
        return pltpu.make_async_remote_copy(
            src_ref=total.at[peer[d]], dst_ref=parts.at[peer[d] if receive else me], send_sem=part_send.at[d],
            recv_sem=part_recv.at[d], device_id=target(d), device_id_type=MESH)

    fetches = [(j, f) for j in range(per) for f in range(len(distant))]
    for j, f in fetches:
        fetch_copy(0, j, f).start()
    for d in range(1, n):
        list_copy(d).start()

    @pl.when(jnp.logical_not(inner))
    def _():
        outer_copy.start()

    for m in range(1, len(FETCHED)):
        for j, f in fetches:
            fetch_copy(FETCHED[m][0], j, f).start()
    if SHIFT:
        shifted(lambda g, items: [fetch_copy(last, *item).start() for item in items])

    for d in distant:
        for group in range(len(GROUPS)):
            held[group][peer[d]] = jnp.zeros_like(held[group][peer[d]])
    chosen[...] = jnp.zeros_like(chosen)
    both[...] = jnp.zeros_like(both)
    def local_pair(code):
        return lax.rem(jnp.maximum(code, 0), local)

    def place(q, code):
        e = local_pair(code)
        if q == last and SHIFT:
            return sum(jnp.where(e == c, at, 0) for at, c in enumerate(order))
        return e

    def column(p, slot, code):
        return p * local + local_pair(code)

    pieces = [(group, d) for group in range(len(GROUPS)) for d in near + (0,)]

    def send_near(count):
        for group, d in pieces[:count]:
            for k in range(GROUPS[group][1]):
                slot = GROUPS[group][0] + k
                code = listed[peer[d], 0, slot] if d else tasks_ref[0, slot]
                at = column(peer[d], slot, code)
                to = sent[group] if d else held[group]
                for row in range(own_rows):
                    to[peer[d], k, pl.ds(row, 1), :] = amp[row, pl.ds(at, 1), spans[group]]
            if d:
                near_copy(group, d).start()
        del pieces[:count]

    def send_tail():
        for f, d in enumerate(distant):
            for slot in range(slots):
                at = column(peer[d], slot, listed[peer[d], 0, slot])
                for row in range(own_rows):
                    tail_sent[f, slot, pl.ds(row, 1), :] = amp[row, pl.ds(at, 1), pl.ds(shared, tail)]
            tail_copy(f).start()


    def fetched(q):
        if q == last and SHIFT:
            def act(g, items):
                for item in items:
                    fetch_copy(q, *item).wait_recv()
                if g == layers - 1:
                    second_copy(q, g).start()
                own_copy(q, g).start()

            shifted(act)
            return

        if q == FETCHED[home[q]][0]:
            for j, f in fetches:
                fetch_copy(q, j, f).wait_recv()

        @pl.when(jnp.logical_not(inner))
        def _():
            second_copy(q).start()

        own_copy(q).start()

    def select(q):
        @pl.when(inner)
        def _():
            if q == last and SHIFT:
                for g in (1, 2):
                    @pl.when(grp == g)
                    def _():
                        for block in (3 - g, 3):
                            layer_copy(block, q, own_send, inward).wait_recv()
            else:
                for block in (outward, inward, second):
                    layer_copy(block, q, own_send, inward).wait_recv()
            if q in home:
                far[q][pl.ds(grp * per, per)] = landing[home[q]][:, :, :, landed(q)]
            for slot in range(slots):
                pick_sent[q][slot] = far[q][place(q, outer_list[0, slot])]
            pick_copy(q, outward).start()

    def near_part(group):
        for d in near:
            near_copy(group, d, True).wait_recv()
        for k in range(GROUPS[group][1]):
            slot = GROUPS[group][0] + k
            both[slot] += multiply(rows[slot, :, spans[group]], held[group][:, k])

    def far_part(q):
        @pl.when(inner)
        def _():
            for slot in range(slots):
                for f, d in enumerate(distant):
                    chosen[slot, peer[d], :, :CHUNKS[q]] = far[q][place(q, tasks_ref[0, slot]), f]

        @pl.when(jnp.logical_not(inner))
        def _():
            pick_copy(q, inward).wait_recv()
            for slot in range(slots):
                for f, d in enumerate(distant):
                    chosen[slot, peer[d], :, :CHUNKS[q]] = pick_held[q][slot, f]

        for slot in range(slots):
            both[slot] += multiply(rows[slot, :, pl.ds(starts[q], CHUNKS[q])], chosen[slot, :, :, :CHUNKS[q]])

    def tail_part():
        for f in range(len(distant)):
            tail_copy(f).wait_recv()
        for slot in range(slots):
            for f, d in enumerate(distant):
                chosen[slot, peer[d], :, :tail] = tail_held[f, slot]
            both[slot] += multiply(rows[slot, :, pl.ds(shared, tail)], chosen[slot, :, :, :tail])

    @pl.when(inner)
    def _():
        outer_copy.wait_recv()

    fetched(0)
    load_amp.wait()
    for d in range(1, n):
        list_copy(d, True).wait_recv()
    send_near(STEP)
    fetched(1)
    send_near(STEP)
    select(0)
    load_int.start()
    for q in range(2, chunks):
        send_near(2)
        fetched(q)
        if q == 2 and tail:
            send_tail()
        if q < last:
            select(q - 1)
    send_near(len(pieces))
    load_int.wait()

    @pl.loop(0, slots)
    def _(slot):
        rows[slot] = split(blocks[slot])

    for q in range(max(1, last - 1), chunks):
        select(q)
    for d in range(1, n):
        list_copy(d).wait_send()
    for q in range(chunks - SHIFT):
        if q == FETCHED[home[q]][0]:
            for j, f in fetches:
                fetch_copy(q, j, f).wait_send()
        own_copy(q).wait_send()
    if SHIFT:
        shifted(lambda g, items: [fetch_copy(last, *item).wait_send() for item in items]
                + [own_copy(last, g).wait_send()])
    for q in range(EARLY):
        far_part(q)
    near_part(0)
    for q in range(EARLY, chunks):
        far_part(q)
    if tail:
        tail_part()
    totals = functools.partial(tile_totals, tasks_ref, both, total, n, local, width, out_ref.shape[0], pack)
    last_slot = GROUPS[-1][0]
    totals(range(last_slot))
    for d in near:
        near_copy(0, d).wait_send()
    for group in range(1, len(GROUPS)):
        near_part(group)
    totals(range(last_slot, slots), True)
    for d in (6, 7, 2, 4, 3, 5, 1):
        part_copy(d).start()
    parts[me] = total[me]
    for group in range(1, len(GROUPS)):
        for d in near:
            near_copy(group, d).wait_send()
    if tail:
        for f in range(len(distant)):
            tail_copy(f).wait_send()

    @pl.when(inner)
    def _():
        for q in range(chunks):
            pick_copy(q, outward).wait_send()

    @pl.when(jnp.logical_not(inner))
    def _():
        outer_copy.wait_send()
        for q in range(chunks - SHIFT):
            second_copy(q).wait_send()

    if SHIFT:
        @pl.when(grp == layers - 1)
        def _():
            second_copy(last, layers - 1).wait_send()

    for d in (1, 2, 4, 3, 5, 6, 7):
        part_copy(d).wait_send()
    for d in (1, 2, 4, 3, 5, 6, 7):
        part_copy(d, True).wait_recv()
    write_sum(parts, out_ref, pack)


def direct_kernel(n, columns, pack, tasks_ref, amp_ref, int_ref, out_ref, listed, amp, blocks, rows, sent, held, both,
                  total, parts, local_sem, list_send, list_recv, send_sem, recv_sem, part_send, part_recv):
    me = lax.axis_index("pair")
    grp = lax.axis_index("grp")
    own_rows, pairs, depth = amp_ref.shape
    slots, width, _ = int_ref.shape
    local = pairs // n
    lists = columns < local

    load_amp = pltpu.make_async_copy(amp_ref, amp, local_sem.at[0])
    load_int = pltpu.make_async_copy(int_ref, blocks, local_sem.at[1])
    load_amp.start()
    load_int.start()

    def other(d):
        return lax.rem(me + d, n)

    def target(p):
        return (p, grp)

    barrier = pltpu.get_barrier_semaphore()

    @pl.loop(1, n)
    def _(d):
        pl.semaphore_signal(barrier, inc=1, device_id=target(other(d)), device_id_type=MESH)

    pl.semaphore_wait(barrier, n - 1)

    def list_copy(frm, to):
        return pltpu.make_async_remote_copy(
            src_ref=tasks_ref, dst_ref=listed.at[frm], send_sem=list_send.at[to], recv_sem=list_recv.at[frm],
            device_id=target(to), device_id_type=MESH)

    def column_copy(c, frm, to):
        return pltpu.make_async_remote_copy(
            src_ref=sent.at[c, to], dst_ref=held.at[c, frm], send_sem=send_sem.at[c, to],
            recv_sem=recv_sem.at[c, frm], device_id=target(to), device_id_type=MESH)

    def part_copy(frm, to):
        return pltpu.make_async_remote_copy(
            src_ref=total.at[to], dst_ref=parts.at[frm], send_sem=part_send.at[to],
            recv_sem=part_recv.at[frm], device_id=target(to), device_id_type=MESH)

    if lists:
        @pl.loop(1, n)
        def _(d):
            list_copy(me, other(d)).start()

    load_amp.wait()

    if lists:
        @pl.loop(1, n)
        def _(d):
            list_copy(other(d), other(d)).wait_recv()

    def column(p, c, codes):
        if lists:
            return p * local + lax.rem(jnp.maximum(codes(c), 0), local)
        return p * local + c

    for c in range(columns):
        @pl.loop(1, n)
        def _(d):
            p = other(d)
            at = column(p, c, lambda k: listed[p, 0, k])
            for row in range(own_rows):
                sent[c, p, pl.ds(row, 1), :] = amp[row, pl.ds(at, 1), :]

            @pl.when(d > 1)
            def _():
                column_copy(c, me, other(d - 1)).start()

        at = column(me, c, lambda k: tasks_ref[0, k])
        for row in range(own_rows):
            held[c, me, pl.ds(row, 1), :] = amp[row, pl.ds(at, 1), :]
        column_copy(c, me, other(n - 1)).start()

    load_int.wait()

    @pl.loop(0, slots)
    def _(slot):
        rows[slot] = split(blocks[slot])

    def arrive(c):
        @pl.loop(1, n)
        def _(d):
            column_copy(c, other(d), other(d)).wait_recv()

    if lists:
        for slot in range(slots):
            arrive(slot)
            both[slot] = multiply(rows[slot], held[slot])
    else:
        for c in range(columns):
            arrive(c)

        @pl.loop(0, slots)
        def _(slot):
            both[slot] = multiply(rows[slot], held[lax.rem(jnp.maximum(tasks_ref[0, slot], 0), local)])

    tile_totals(tasks_ref, both, total, n, local, width, out_ref.shape[0], pack, range(slots))

    @pl.loop(1, n)
    def _(d):
        part_copy(me, other(d)).start()

    parts[me] = total[me]

    @pl.loop(1, n)
    def _(d):
        part_copy(other(d), other(d)).wait_recv()

    write_sum(parts, out_ref, pack)

    @pl.loop(1, n)
    def _(d):
        part_copy(me, other(d)).wait_send()
        if lists:
            list_copy(me, other(d)).wait_send()
        for c in range(columns):
            column_copy(c, me, other(d)).wait_send()


def body(n, layers, amplitudes, integrals, tasks):
    own_rows, pairs, depth = amplitudes.shape
    slots, width = integrals.shape[2:4]
    local = pairs // n
    columns = min(local, slots)
    part_rows = NT * width // n
    held_rows = n * own_rows
    pack = max(1, 128 // held_rows)
    tail = depth - sum(CHUNKS)
    planes = n == 8 and layers == 4 and local == 8 and slots == 4 and depth == 4096
    dma = pltpu.SemaphoreType.DMA
    scratch = [
        pltpu.SMEM((n, 1, slots), jnp.int32),
        pltpu.VMEM(amplitudes.shape, jnp.float32),
        pltpu.VMEM((slots, width, depth), jnp.float32),
        pltpu.VMEM((slots, 2 * width, depth), jnp.bfloat16),
    ]
    results = [
        pltpu.VMEM((slots, 2 * width, 2 * held_rows), jnp.float32),
        pltpu.VMEM((n, part_rows // pack, held_rows * pack), jnp.float32),
        pltpu.VMEM((n, part_rows // pack, held_rows * pack), jnp.float32),
    ]
    if planes:
        kernel = functools.partial(plane_kernel, layers, pack)
        scratch += [pltpu.VMEM((slots, n, own_rows, max(CHUNKS + (tail,))), jnp.float32)] + results + [
            dma, dma, dma((n,)), dma((n,)), dma((len(GROUPS), n)), dma((len(GROUPS), n)), dma((2,)), dma((2,)),
            dma((len(FETCHED) + 1, 3, 2)), dma((len(FETCHED) + 1, 3, 2)), dma((len(CHUNKS),)), dma((len(CHUNKS),)),
            dma((len(CHUNKS), layers)), dma((len(CHUNKS),)), dma((len(CHUNKS),)), dma((n,)), dma((n,)),
            pltpu.SMEM((1, slots), jnp.int32), dma, dma,
        ]
        scratch += 2 * [pltpu.VMEM((n, count, own_rows, size), jnp.float32) for _, count, _, size in GROUPS]
        scratch += [pltpu.VMEM((local, 2, own_rows, chunk), jnp.float32) for chunk in CHUNKS]
        scratch += 2 * [pltpu.VMEM((slots, 2, own_rows, chunk), jnp.float32) for chunk in CHUNKS]
        if tail:
            scratch += 2 * [pltpu.VMEM((2, slots, own_rows, tail), jnp.float32)]
    else:
        kernel = functools.partial(direct_kernel, n, columns, pack)
        scratch += 2 * [pltpu.VMEM((columns, n, own_rows, depth), jnp.float32)] + results + [
            dma((2,)), dma((n,)), dma((n,)), dma((columns, n)), dma((columns, n)), dma((n,)), dma((n,)),
        ]
    if planes:
        scratch += [pltpu.VMEM((local // layers, 2, own_rows, sum(CHUNKS[q] for q in members)), jnp.float32)
                    for members in FETCHED]
    out = pl.pallas_call(
        kernel,
        out_shape=(pltpu.VMEM if planes else jax.ShapeDtypeStruct)((part_rows, held_rows), jnp.float32),
        in_specs=[
            pl.BlockSpec(memory_space=pltpu.SMEM),
            pl.BlockSpec(memory_space=pl.ANY),
            pl.BlockSpec(memory_space=pl.ANY),
        ],
        out_specs=pl.BlockSpec(memory_space=pltpu.VMEM),
        scratch_shapes=scratch,
        compiler_params=pltpu.CompilerParams(
            collective_id=0, has_side_effects=True, vmem_limit_bytes=60 * 1024 * 1024),
    )(tasks[0], amplitudes, integrals[0, 0])
    return out[None]


def solution(mesh):
    return jax.shard_map(
        functools.partial(body, mesh.shape["pair"], mesh.shape["grp"]),
        mesh=mesh,
        in_specs=(
            P("pair", None, None),
            P("grp", "pair", None, None, None),
            P("grp", "pair", None),
        ),
        out_specs=P("grp", "pair", None),
        check_vma=False,
    )
```

```python
import functools

import jax
import jax.numpy as jnp
from jax import lax
from jax.experimental import pallas as pl
from jax.experimental.pallas import tpu as pltpu
from jax.sharding import PartitionSpec as P

NT = 8
CHUNKS = (384, 512, 640, 768, 768, 640, 384)
FETCHED = ((0,), (1,), (2, 3), (4, 5))
GROUPS = ((0, 4, 0, 3584), (0, 4, 3584, 512))
EARLY = 5
DUTY = ((), (2, 3), (4, 5, 0), (6, 7, 1))
SHIFT = 1
STEP = 1
MESH = pl.DeviceIdType.MESH


def split(x):
    high = x.astype(jnp.bfloat16)
    low = (x - high.astype(jnp.float32)).astype(jnp.bfloat16)
    return jnp.concatenate([high, low], axis=0)


def multiply(rows, operand):
    operand = operand.reshape(-1, operand.shape[-1])
    return lax.dot_general(rows, split(operand), (((1,), (1,)), ((), ())), preferred_element_type=jnp.float32)


def tile_totals(tasks_ref, both, total, n, local, width, part_rows, pack, chosen_slots, more=False):
    piece = part_rows // pack
    tiles, terms = {}, {}
    for slot in chosen_slots:
        code = tasks_ref[0, slot]
        tiles[slot] = jnp.where(code >= 0, lax.div(jnp.maximum(code, 0), local), -1)
        term = both[slot]
        term = term[:width] + term[width:]
        half = term.shape[1] // 2
        terms[slot] = term[:, :half] + term[:, half:]
    packed = {}
    for p in range(n):
        first = p * part_rows
        low = first % width
        value = total[p] if more else jnp.zeros(total.shape[1:], jnp.float32)
        for slot in chosen_slots:
            if (slot, low) not in packed:
                packed[slot, low] = jnp.concatenate(
                    [terms[slot][low + i * piece: low + (i + 1) * piece] for i in range(pack)], axis=1)
            value += jnp.where(tiles[slot] == first // width, packed[slot, low], 0.0)
        total[p] = value


def write_sum(parts, out_ref, pack):
    n = parts.shape[0]
    piece = out_ref.shape[0] // pack
    held_rows = out_ref.shape[1]
    result = parts[0]
    for p in range(1, n):
        result += parts[p]
    for i in range(pack):
        out_ref[i * piece: (i + 1) * piece, :] = result[:, i * held_rows: (i + 1) * held_rows]


def plane_kernel(layers, pack, tasks_ref, amp_ref, int_ref, out_ref, listed, amp, blocks, rows, chosen, both, total,
                 parts, amp_sem, int_sem, list_send, list_recv, near_send, near_recv, tail_send, tail_recv, fetch_send,
                 fetch_recv, own_send, second_send, layer_recv,
                 pick_send, pick_recv, part_send, part_recv, outer_list, outer_send, outer_recv, *buffers):
    n = 8
    me = lax.axis_index("pair")
    grp = lax.axis_index("grp")
    own_rows, pairs, depth = amp_ref.shape
    slots, width, _ = int_ref.shape
    local = pairs // n
    per = local // layers
    shared = sum(CHUNKS)
    tail = depth - shared
    sent, held = buffers[:len(GROUPS)], buffers[len(GROUPS): 2 * len(GROUPS)]
    far = buffers[2 * len(GROUPS): 2 * len(GROUPS) + len(CHUNKS)]
    used = 2 * len(GROUPS) + len(CHUNKS)
    pick_sent, pick_held = buffers[used: used + len(CHUNKS)], buffers[used + len(CHUNKS): used + 2 * len(CHUNKS)]
    tail_sent, tail_held = buffers[-2 - len(FETCHED): -len(FETCHED)] if tail else (None, None)
    starts = [sum(CHUNKS[:q]) for q in range(len(CHUNKS))]
    spans = [pl.ds(start, size) for _, _, start, size in GROUPS]

    def bit(value, d):
        return value if not d else 1 - value

    core, x, y = lax.rem(me, 2), lax.rem(me // 2, 2), me // 4
    peer = [bit(y, d // 4) * 4 + bit(x, d // 2 % 2) * 2 + bit(core, d % 2) for d in range(n)]
    near = (2, 4, 3, 5, 1)
    chunks = len(CHUNKS)
    last = chunks - 1
    order = sum(DUTY, ())
    landing = buffers[len(buffers) - len(FETCHED):]
    home = {q: m for m, held_chunks in enumerate(FETCHED) for q in held_chunks}
    distant = (6, 7)
    inner = (grp >= 1) & (grp <= 2)
    inward = lax.rem(grp, 2) + 1
    outward = (grp - 1) * 3
    second = jnp.where(inner, 3 - outward, 3 - inward)

    def target(d):
        return (peer[d], grp)

    load_amp = pltpu.make_async_copy(amp_ref, amp, amp_sem)
    load_int = pltpu.make_async_copy(int_ref, blocks, int_sem)
    load_amp.start()

    barrier = pltpu.get_barrier_semaphore()
    pl.semaphore_signal(barrier, inc=1, device_id=(me, second), device_id_type=MESH)
    for d in (6, 7, 2, 4, 3, 5, 1):
        pl.semaphore_signal(barrier, inc=1, device_id=target(d), device_id_type=MESH)
    pl.semaphore_signal(barrier, inc=1, device_id=(me, inward), device_id_type=MESH)

    @pl.when(inner)
    def _():
        pl.semaphore_signal(barrier, inc=1, device_id=(me, outward), device_id_type=MESH)

    pl.semaphore_wait(barrier, n + 1 + jnp.where(inner, 1, 0))

    def list_copy(d, receive=False):
        return pltpu.make_async_remote_copy(
            src_ref=tasks_ref, dst_ref=listed.at[peer[d] if receive else me], send_sem=list_send.at[d],
            recv_sem=list_recv.at[d], device_id=target(d), device_id_type=MESH)

    def near_copy(group, d, receive=False):
        return pltpu.make_async_remote_copy(
            src_ref=sent[group].at[peer[d]], dst_ref=held[group].at[peer[d] if receive else me],
            send_sem=near_send.at[group, d], recv_sem=near_recv.at[group, d], device_id=target(d),
            device_id_type=MESH)

    def tail_copy(f):
        return pltpu.make_async_remote_copy(
            src_ref=tail_sent.at[f], dst_ref=tail_held.at[f], send_sem=tail_send.at[f], recv_sem=tail_recv.at[f],
            device_id=target(distant[f]), device_id_type=MESH)

    def fetch_copy(q, j, f, column=None, at=None):
        if column is None:
            m = home[q]
            column, start, size, to = grp * per + j, starts[FETCHED[m][0]], landing[m].shape[-1], landing[m].at[j, f]
        else:
            m, start, size, to = len(FETCHED), starts[q], CHUNKS[q], far[q].at[at, f]
        return pltpu.make_async_remote_copy(
            src_ref=amp_ref.at[:, peer[distant[f]] * local + column, pl.ds(start, size)], dst_ref=to,
            send_sem=fetch_send.at[m, j, f], recv_sem=fetch_recv.at[m, j, f], device_id=target(distant[f]),
            device_id_type=MESH)

    def landed(q):
        return pl.ds(starts[q] - starts[FETCHED[home[q]][0]], CHUNKS[q])

    def layer_copy(block, q, send, to, own=False):
        if q == last and SHIFT:
            at = far[q].at[pl.ds(order.index(DUTY[block][0]), len(DUTY[block]))]
        else:
            at = far[q].at[pl.ds(block * per, per)]
        frm = landing[home[q]].at[:, :, :, landed(q)] if own and q in home else at
        return pltpu.make_async_remote_copy(
            src_ref=frm, dst_ref=at, send_sem=send.at[q], recv_sem=layer_recv.at[q, block], device_id=(me, to),
            device_id_type=MESH)

    def own_copy(q, block=None):
        return layer_copy(grp if block is None else block, q, own_send, inward, True)

    def second_copy(q, block=None):
        return layer_copy(grp if block is None else block, q, second_send, second, True)

    def shifted(act):
        for g, columns in enumerate(DUTY):
            if columns:
                @pl.when(grp == g)
                def _():
                    act(g, [(j, f, e, order.index(e)) for j, e in enumerate(columns) for f in range(len(distant))])

    def pick_copy(q, to):
        return pltpu.make_async_remote_copy(
            src_ref=pick_sent[q], dst_ref=pick_held[q], send_sem=pick_send.at[q], recv_sem=pick_recv.at[q],
            device_id=(me, to), device_id_type=MESH)

    outer_copy = pltpu.make_async_remote_copy(
        src_ref=tasks_ref, dst_ref=outer_list, send_sem=outer_send, recv_sem=outer_recv, device_id=(me, inward),
        device_id_type=MESH)

    def part_copy(d, receive=False):
        return pltpu.make_async_remote_copy(
            src_ref=total.at[peer[d]], dst_ref=parts.at[peer[d] if receive else me], send_sem=part_send.at[d],
            recv_sem=part_recv.at[d], device_id=target(d), device_id_type=MESH)

    fetches = [(j, f) for j in range(per) for f in range(len(distant))]
    for j, f in fetches:
        fetch_copy(0, j, f).start()
    for d in range(1, n):
        list_copy(d).start()

    @pl.when(jnp.logical_not(inner))
    def _():
        outer_copy.start()

    for m in range(1, len(FETCHED)):
        for j, f in fetches:
            fetch_copy(FETCHED[m][0], j, f).start()
    if SHIFT:
        shifted(lambda g, items: [fetch_copy(last, *item).start() for item in items])

    for d in distant:
        for group in range(len(GROUPS)):
            held[group][peer[d]] = jnp.zeros_like(held[group][peer[d]])
    chosen[...] = jnp.zeros_like(chosen)
    both[...] = jnp.zeros_like(both)
    def local_pair(code):
        return lax.rem(jnp.maximum(code, 0), local)

    def place(q, code):
        e = local_pair(code)
        if q == last and SHIFT:
            return sum(jnp.where(e == c, at, 0) for at, c in enumerate(order))
        return e

    def column(p, slot, code):
        return p * local + local_pair(code)

    pieces = [(group, d) for group in range(len(GROUPS)) for d in near + (0,)]

    def send_near(count):
        for group, d in pieces[:count]:
            for k in range(GROUPS[group][1]):
                slot = GROUPS[group][0] + k
                code = listed[peer[d], 0, slot] if d else tasks_ref[0, slot]
                at = column(peer[d], slot, code)
                to = sent[group] if d else held[group]
                for row in range(own_rows):
                    to[peer[d], k, pl.ds(row, 1), :] = amp[row, pl.ds(at, 1), spans[group]]
            if d:
                near_copy(group, d).start()
        del pieces[:count]

    def send_tail():
        for f, d in enumerate(distant):
            for slot in range(slots):
                at = column(peer[d], slot, listed[peer[d], 0, slot])
                for row in range(own_rows):
                    tail_sent[f, slot, pl.ds(row, 1), :] = amp[row, pl.ds(at, 1), pl.ds(shared, tail)]
            tail_copy(f).start()


    def fetched(q):
        if q == last and SHIFT:
            def act(g, items):
                for item in items:
                    fetch_copy(q, *item).wait_recv()
                if g == layers - 1:
                    second_copy(q, g).start()
                own_copy(q, g).start()

            shifted(act)
            return

        if q == FETCHED[home[q]][0]:
            for j, f in fetches:
                fetch_copy(q, j, f).wait_recv()

        @pl.when(jnp.logical_not(inner))
        def _():
            second_copy(q).start()

        own_copy(q).start()

    def select(q):
        @pl.when(inner)
        def _():
            if q == last and SHIFT:
                for g in (1, 2):
                    @pl.when(grp == g)
                    def _():
                        for block in (3 - g, 3):
                            layer_copy(block, q, own_send, inward).wait_recv()
            else:
                for block in (outward, inward, second):
                    layer_copy(block, q, own_send, inward).wait_recv()
            if q in home:
                far[q][pl.ds(grp * per, per)] = landing[home[q]][:, :, :, landed(q)]
            for slot in range(slots):
                pick_sent[q][slot] = far[q][place(q, outer_list[0, slot])]
            pick_copy(q, outward).start()

    def near_part(group):
        for d in near:
            near_copy(group, d, True).wait_recv()
        for k in range(GROUPS[group][1]):
            slot = GROUPS[group][0] + k
            both[slot] += multiply(rows[slot, :, spans[group]], held[group][:, k])

    def far_part(q):
        @pl.when(inner)
        def _():
            for slot in range(slots):
                for f, d in enumerate(distant):
                    chosen[slot, peer[d], :, :CHUNKS[q]] = far[q][place(q, tasks_ref[0, slot]), f]

        @pl.when(jnp.logical_not(inner))
        def _():
            pick_copy(q, inward).wait_recv()
            for slot in range(slots):
                for f, d in enumerate(distant):
                    chosen[slot, peer[d], :, :CHUNKS[q]] = pick_held[q][slot, f]

        for slot in range(slots):
            both[slot] += multiply(rows[slot, :, pl.ds(starts[q], CHUNKS[q])], chosen[slot, :, :, :CHUNKS[q]])

    def tail_part():
        for f in range(len(distant)):
            tail_copy(f).wait_recv()
        for slot in range(slots):
            for f, d in enumerate(distant):
                chosen[slot, peer[d], :, :tail] = tail_held[f, slot]
            both[slot] += multiply(rows[slot, :, pl.ds(shared, tail)], chosen[slot, :, :, :tail])

    @pl.when(inner)
    def _():
        outer_copy.wait_recv()

    fetched(0)
    load_amp.wait()
    for d in range(1, n):
        list_copy(d, True).wait_recv()
    fetched(1)
    send_near(STEP)
    select(0)
    send_near(STEP)
    load_int.start()
    for q in range(2, chunks):
        send_near(2)
        fetched(q)
        if q == 2 and tail:
            send_tail()
        if q < last:
            select(q - 1)
    send_near(len(pieces))
    load_int.wait()

    @pl.loop(0, slots)
    def _(slot):
        rows[slot] = split(blocks[slot])

    for q in range(max(1, last - 1), chunks):
        select(q)
    for d in range(1, n):
        list_copy(d).wait_send()
    for q in range(chunks - SHIFT):
        if q == FETCHED[home[q]][0]:
            for j, f in fetches:
                fetch_copy(q, j, f).wait_send()
        own_copy(q).wait_send()
    if SHIFT:
        shifted(lambda g, items: [fetch_copy(last, *item).wait_send() for item in items]
                + [own_copy(last, g).wait_send()])
    for q in range(EARLY):
        far_part(q)
    near_part(0)
    for q in range(EARLY, chunks):
        far_part(q)
    if tail:
        tail_part()
    totals = functools.partial(tile_totals, tasks_ref, both, total, n, local, width, out_ref.shape[0], pack)
    last_slot = GROUPS[-1][0]
    totals(range(last_slot))
    for d in near:
        near_copy(0, d).wait_send()
    for group in range(1, len(GROUPS)):
        near_part(group)
    totals(range(last_slot, slots), True)
    for d in (6, 7, 2, 4, 3, 5, 1):
        part_copy(d).start()
    parts[me] = total[me]
    for group in range(1, len(GROUPS)):
        for d in near:
            near_copy(group, d).wait_send()
    if tail:
        for f in range(len(distant)):
            tail_copy(f).wait_send()

    @pl.when(inner)
    def _():
        for q in range(chunks):
            pick_copy(q, outward).wait_send()

    @pl.when(jnp.logical_not(inner))
    def _():
        outer_copy.wait_send()
        for q in range(chunks - SHIFT):
            second_copy(q).wait_send()

    if SHIFT:
        @pl.when(grp == layers - 1)
        def _():
            second_copy(last, layers - 1).wait_send()

    for d in (1, 2, 4, 3, 5, 6, 7):
        part_copy(d).wait_send()
    for d in (1, 2, 4, 3, 5, 6, 7):
        part_copy(d, True).wait_recv()
    write_sum(parts, out_ref, pack)


def direct_kernel(n, columns, pack, tasks_ref, amp_ref, int_ref, out_ref, listed, amp, blocks, rows, sent, held, both,
                  total, parts, local_sem, list_send, list_recv, send_sem, recv_sem, part_send, part_recv):
    me = lax.axis_index("pair")
    grp = lax.axis_index("grp")
    own_rows, pairs, depth = amp_ref.shape
    slots, width, _ = int_ref.shape
    local = pairs // n
    lists = columns < local

    load_amp = pltpu.make_async_copy(amp_ref, amp, local_sem.at[0])
    load_int = pltpu.make_async_copy(int_ref, blocks, local_sem.at[1])
    load_amp.start()
    load_int.start()

    def other(d):
        return lax.rem(me + d, n)

    def target(p):
        return (p, grp)

    barrier = pltpu.get_barrier_semaphore()

    @pl.loop(1, n)
    def _(d):
        pl.semaphore_signal(barrier, inc=1, device_id=target(other(d)), device_id_type=MESH)

    pl.semaphore_wait(barrier, n - 1)

    def list_copy(frm, to):
        return pltpu.make_async_remote_copy(
            src_ref=tasks_ref, dst_ref=listed.at[frm], send_sem=list_send.at[to], recv_sem=list_recv.at[frm],
            device_id=target(to), device_id_type=MESH)

    def column_copy(c, frm, to):
        return pltpu.make_async_remote_copy(
            src_ref=sent.at[c, to], dst_ref=held.at[c, frm], send_sem=send_sem.at[c, to],
            recv_sem=recv_sem.at[c, frm], device_id=target(to), device_id_type=MESH)

    def part_copy(frm, to):
        return pltpu.make_async_remote_copy(
            src_ref=total.at[to], dst_ref=parts.at[frm], send_sem=part_send.at[to],
            recv_sem=part_recv.at[frm], device_id=target(to), device_id_type=MESH)

    if lists:
        @pl.loop(1, n)
        def _(d):
            list_copy(me, other(d)).start()

    load_amp.wait()

    if lists:
        @pl.loop(1, n)
        def _(d):
            list_copy(other(d), other(d)).wait_recv()

    def column(p, c, codes):
        if lists:
            return p * local + lax.rem(jnp.maximum(codes(c), 0), local)
        return p * local + c

    for c in range(columns):
        @pl.loop(1, n)
        def _(d):
            p = other(d)
            at = column(p, c, lambda k: listed[p, 0, k])
            for row in range(own_rows):
                sent[c, p, pl.ds(row, 1), :] = amp[row, pl.ds(at, 1), :]

            @pl.when(d > 1)
            def _():
                column_copy(c, me, other(d - 1)).start()

        at = column(me, c, lambda k: tasks_ref[0, k])
        for row in range(own_rows):
            held[c, me, pl.ds(row, 1), :] = amp[row, pl.ds(at, 1), :]
        column_copy(c, me, other(n - 1)).start()

    load_int.wait()

    @pl.loop(0, slots)
    def _(slot):
        rows[slot] = split(blocks[slot])

    def arrive(c):
        @pl.loop(1, n)
        def _(d):
            column_copy(c, other(d), other(d)).wait_recv()

    if lists:
        for slot in range(slots):
            arrive(slot)
            both[slot] = multiply(rows[slot], held[slot])
    else:
        for c in range(columns):
            arrive(c)

        @pl.loop(0, slots)
        def _(slot):
            both[slot] = multiply(rows[slot], held[lax.rem(jnp.maximum(tasks_ref[0, slot], 0), local)])

    tile_totals(tasks_ref, both, total, n, local, width, out_ref.shape[0], pack, range(slots))

    @pl.loop(1, n)
    def _(d):
        part_copy(me, other(d)).start()

    parts[me] = total[me]

    @pl.loop(1, n)
    def _(d):
        part_copy(other(d), other(d)).wait_recv()

    write_sum(parts, out_ref, pack)

    @pl.loop(1, n)
    def _(d):
        part_copy(me, other(d)).wait_send()
        if lists:
            list_copy(me, other(d)).wait_send()
        for c in range(columns):
            column_copy(c, me, other(d)).wait_send()


def body(n, layers, amplitudes, integrals, tasks):
    own_rows, pairs, depth = amplitudes.shape
    slots, width = integrals.shape[2:4]
    local = pairs // n
    columns = min(local, slots)
    part_rows = NT * width // n
    held_rows = n * own_rows
    pack = max(1, 128 // held_rows)
    tail = depth - sum(CHUNKS)
    planes = n == 8 and layers == 4 and local == 8 and slots == 4 and depth == 4096
    dma = pltpu.SemaphoreType.DMA
    scratch = [
        pltpu.SMEM((n, 1, slots), jnp.int32),
        pltpu.VMEM(amplitudes.shape, jnp.float32),
        pltpu.VMEM((slots, width, depth), jnp.float32),
        pltpu.VMEM((slots, 2 * width, depth), jnp.bfloat16),
    ]
    results = [
        pltpu.VMEM((slots, 2 * width, 2 * held_rows), jnp.float32),
        pltpu.VMEM((n, part_rows // pack, held_rows * pack), jnp.float32),
        pltpu.VMEM((n, part_rows // pack, held_rows * pack), jnp.float32),
    ]
    if planes:
        kernel = functools.partial(plane_kernel, layers, pack)
        scratch += [pltpu.VMEM((slots, n, own_rows, max(CHUNKS + (tail,))), jnp.float32)] + results + [
            dma, dma, dma((n,)), dma((n,)), dma((len(GROUPS), n)), dma((len(GROUPS), n)), dma((2,)), dma((2,)),
            dma((len(FETCHED) + 1, 3, 2)), dma((len(FETCHED) + 1, 3, 2)), dma((len(CHUNKS),)), dma((len(CHUNKS),)),
            dma((len(CHUNKS), layers)), dma((len(CHUNKS),)), dma((len(CHUNKS),)), dma((n,)), dma((n,)),
            pltpu.SMEM((1, slots), jnp.int32), dma, dma,
        ]
        scratch += 2 * [pltpu.VMEM((n, count, own_rows, size), jnp.float32) for _, count, _, size in GROUPS]
        scratch += [pltpu.VMEM((local, 2, own_rows, chunk), jnp.float32) for chunk in CHUNKS]
        scratch += 2 * [pltpu.VMEM((slots, 2, own_rows, chunk), jnp.float32) for chunk in CHUNKS]
        if tail:
            scratch += 2 * [pltpu.VMEM((2, slots, own_rows, tail), jnp.float32)]
    else:
        kernel = functools.partial(direct_kernel, n, columns, pack)
        scratch += 2 * [pltpu.VMEM((columns, n, own_rows, depth), jnp.float32)] + results + [
            dma((2,)), dma((n,)), dma((n,)), dma((columns, n)), dma((columns, n)), dma((n,)), dma((n,)),
        ]
    if planes:
        scratch += [pltpu.VMEM((local // layers, 2, own_rows, sum(CHUNKS[q] for q in members)), jnp.float32)
                    for members in FETCHED]
    out = pl.pallas_call(
        kernel,
        out_shape=(pltpu.VMEM if planes else jax.ShapeDtypeStruct)((part_rows, held_rows), jnp.float32),
        in_specs=[
            pl.BlockSpec(memory_space=pltpu.SMEM),
            pl.BlockSpec(memory_space=pl.ANY),
            pl.BlockSpec(memory_space=pl.ANY),
        ],
        out_specs=pl.BlockSpec(memory_space=pltpu.VMEM),
        scratch_shapes=scratch,
        compiler_params=pltpu.CompilerParams(
            collective_id=0, has_side_effects=True, vmem_limit_bytes=60 * 1024 * 1024),
    )(tasks[0], amplitudes, integrals[0, 0])
    return out[None]


def solution(mesh):
    return jax.shard_map(
        functools.partial(body, mesh.shape["pair"], mesh.shape["grp"]),
        mesh=mesh,
        in_specs=(
            P("pair", None, None),
            P("grp", "pair", None, None, None),
            P("grp", "pair", None),
        ),
        out_specs=P("grp", "pair", None),
        check_vma=False,
    )
```

```python
import functools

import jax
import jax.numpy as jnp
from jax import lax
from jax.experimental import pallas as pl
from jax.experimental.pallas import tpu as pltpu
from jax.sharding import PartitionSpec as P

NT = 8
CHUNKS = (384, 512, 640, 768, 768, 640, 384)
FETCHED = ((0,), (1,), (2, 3), (4, 5))
GROUPS = ((0, 4, 0, 3584), (0, 4, 3584, 512))
EARLY = 5
DUTY = ((), (2, 3), (4, 5, 0), (6, 7, 1))
SHIFT = 1
STEP = 1
MESH = pl.DeviceIdType.MESH


def split(x):
    high = x.astype(jnp.bfloat16)
    low = (x - high.astype(jnp.float32)).astype(jnp.bfloat16)
    return jnp.concatenate([high, low], axis=0)


def multiply(rows, operand):
    operand = operand.reshape(-1, operand.shape[-1])
    return lax.dot_general(rows, split(operand), (((1,), (1,)), ((), ())), preferred_element_type=jnp.float32)


def tile_totals(tasks_ref, both, total, n, local, width, part_rows, pack, chosen_slots, more=False):
    piece = part_rows // pack
    tiles, terms = {}, {}
    for slot in chosen_slots:
        code = tasks_ref[0, slot]
        tiles[slot] = jnp.where(code >= 0, lax.div(jnp.maximum(code, 0), local), -1)
        term = both[slot]
        term = term[:width] + term[width:]
        half = term.shape[1] // 2
        terms[slot] = term[:, :half] + term[:, half:]
    packed = {}
    for p in range(n):
        first = p * part_rows
        low = first % width
        value = total[p] if more else jnp.zeros(total.shape[1:], jnp.float32)
        for slot in chosen_slots:
            if (slot, low) not in packed:
                packed[slot, low] = jnp.concatenate(
                    [terms[slot][low + i * piece: low + (i + 1) * piece] for i in range(pack)], axis=1)
            value += jnp.where(tiles[slot] == first // width, packed[slot, low], 0.0)
        total[p] = value


def write_sum(parts, out_ref, pack):
    n = parts.shape[0]
    piece = out_ref.shape[0] // pack
    held_rows = out_ref.shape[1]
    result = parts[0]
    for p in range(1, n):
        result += parts[p]
    for i in range(pack):
        out_ref[i * piece: (i + 1) * piece, :] = result[:, i * held_rows: (i + 1) * held_rows]


def plane_kernel(layers, pack, tasks_ref, amp_ref, int_ref, out_ref, listed, amp, blocks, rows, chosen, both, total,
                 parts, amp_sem, int_sem, list_send, list_recv, near_send, near_recv, tail_send, tail_recv, fetch_send,
                 fetch_recv, own_send, second_send, layer_recv,
                 pick_send, pick_recv, part_send, part_recv, outer_list, outer_send, outer_recv, *buffers):
    n = 8
    me = lax.axis_index("pair")
    grp = lax.axis_index("grp")
    own_rows, pairs, depth = amp_ref.shape
    slots, width, _ = int_ref.shape
    local = pairs // n
    per = local // layers
    shared = sum(CHUNKS)
    tail = depth - shared
    sent, held = buffers[:len(GROUPS)], buffers[len(GROUPS): 2 * len(GROUPS)]
    far = buffers[2 * len(GROUPS): 2 * len(GROUPS) + len(CHUNKS)]
    used = 2 * len(GROUPS) + len(CHUNKS)
    pick_sent, pick_held = buffers[used: used + len(CHUNKS)], buffers[used + len(CHUNKS): used + 2 * len(CHUNKS)]
    tail_sent, tail_held = buffers[-2 - len(FETCHED): -len(FETCHED)] if tail else (None, None)
    starts = [sum(CHUNKS[:q]) for q in range(len(CHUNKS))]
    spans = [pl.ds(start, size) for _, _, start, size in GROUPS]

    def bit(value, d):
        return value if not d else 1 - value

    core, x, y = lax.rem(me, 2), lax.rem(me // 2, 2), me // 4
    peer = [bit(y, d // 4) * 4 + bit(x, d // 2 % 2) * 2 + bit(core, d % 2) for d in range(n)]
    near = (2, 4, 3, 5, 1)
    chunks = len(CHUNKS)
    last = chunks - 1
    order = sum(DUTY, ())
    landing = buffers[len(buffers) - len(FETCHED):]
    home = {q: m for m, held_chunks in enumerate(FETCHED) for q in held_chunks}
    distant = (6, 7)
    inner = (grp >= 1) & (grp <= 2)
    inward = lax.rem(grp, 2) + 1
    outward = (grp - 1) * 3
    second = jnp.where(inner, 3 - outward, 3 - inward)

    def target(d):
        return (peer[d], grp)

    load_amp = pltpu.make_async_copy(amp_ref, amp, amp_sem)
    load_int = pltpu.make_async_copy(int_ref, blocks, int_sem)
    load_amp.start()

    barrier = pltpu.get_barrier_semaphore()
    pl.semaphore_signal(barrier, inc=1, device_id=(me, second), device_id_type=MESH)
    for d in (6, 7, 2, 4, 3, 5, 1):
        pl.semaphore_signal(barrier, inc=1, device_id=target(d), device_id_type=MESH)
    pl.semaphore_signal(barrier, inc=1, device_id=(me, inward), device_id_type=MESH)

    @pl.when(inner)
    def _():
        pl.semaphore_signal(barrier, inc=1, device_id=(me, outward), device_id_type=MESH)

    pl.semaphore_wait(barrier, n + 1 + jnp.where(inner, 1, 0))

    def list_copy(d, receive=False):
        return pltpu.make_async_remote_copy(
            src_ref=tasks_ref, dst_ref=listed.at[peer[d] if receive else me], send_sem=list_send.at[d],
            recv_sem=list_recv.at[d], device_id=target(d), device_id_type=MESH)

    def near_copy(group, d, receive=False):
        return pltpu.make_async_remote_copy(
            src_ref=sent[group].at[peer[d]], dst_ref=held[group].at[peer[d] if receive else me],
            send_sem=near_send.at[group, d], recv_sem=near_recv.at[group, d], device_id=target(d),
            device_id_type=MESH)

    def tail_copy(f):
        return pltpu.make_async_remote_copy(
            src_ref=tail_sent.at[f], dst_ref=tail_held.at[f], send_sem=tail_send.at[f], recv_sem=tail_recv.at[f],
            device_id=target(distant[f]), device_id_type=MESH)

    def fetch_copy(q, j, f, column=None, at=None):
        if column is None:
            m = home[q]
            column, start, size, to = grp * per + j, starts[FETCHED[m][0]], landing[m].shape[-1], landing[m].at[j, f]
        else:
            m, start, size, to = len(FETCHED), starts[q], CHUNKS[q], far[q].at[at, f]
        return pltpu.make_async_remote_copy(
            src_ref=amp_ref.at[:, peer[distant[f]] * local + column, pl.ds(start, size)], dst_ref=to,
            send_sem=fetch_send.at[m, j, f], recv_sem=fetch_recv.at[m, j, f], device_id=target(distant[f]),
            device_id_type=MESH)

    def landed(q):
        return pl.ds(starts[q] - starts[FETCHED[home[q]][0]], CHUNKS[q])

    def layer_copy(block, q, send, to, own=False):
        if q == last and SHIFT:
            at = far[q].at[pl.ds(order.index(DUTY[block][0]), len(DUTY[block]))]
        else:
            at = far[q].at[pl.ds(block * per, per)]
        frm = landing[home[q]].at[:, :, :, landed(q)] if own and q in home else at
        return pltpu.make_async_remote_copy(
            src_ref=frm, dst_ref=at, send_sem=send.at[q], recv_sem=layer_recv.at[q, block], device_id=(me, to),
            device_id_type=MESH)

    def own_copy(q, block=None):
        return layer_copy(grp if block is None else block, q, own_send, inward, True)

    def second_copy(q, block=None):
        return layer_copy(grp if block is None else block, q, second_send, second, True)

    def shifted(act):
        for g, columns in enumerate(DUTY):
            if columns:
                @pl.when(grp == g)
                def _():
                    act(g, [(j, f, e, order.index(e)) for j, e in enumerate(columns) for f in range(len(distant))])

    def pick_copy(q, to):
        return pltpu.make_async_remote_copy(
            src_ref=pick_sent[q], dst_ref=pick_held[q], send_sem=pick_send.at[q], recv_sem=pick_recv.at[q],
            device_id=(me, to), device_id_type=MESH)

    outer_copy = pltpu.make_async_remote_copy(
        src_ref=tasks_ref, dst_ref=outer_list, send_sem=outer_send, recv_sem=outer_recv, device_id=(me, inward),
        device_id_type=MESH)

    def part_copy(d, receive=False):
        return pltpu.make_async_remote_copy(
            src_ref=total.at[peer[d]], dst_ref=parts.at[peer[d] if receive else me], send_sem=part_send.at[d],
            recv_sem=part_recv.at[d], device_id=target(d), device_id_type=MESH)

    fetches = [(j, f) for j in range(per) for f in range(len(distant))]
    for j, f in fetches:
        fetch_copy(0, j, f).start()
    for d in range(1, n):
        list_copy(d).start()

    @pl.when(jnp.logical_not(inner))
    def _():
        outer_copy.start()

    for m in range(1, len(FETCHED)):
        for j, f in fetches:
            fetch_copy(FETCHED[m][0], j, f).start()
    if SHIFT:
        shifted(lambda g, items: [fetch_copy(last, *item).start() for item in items])

    for d in distant:
        for group in range(len(GROUPS)):
            held[group][peer[d]] = jnp.zeros_like(held[group][peer[d]])
    chosen[...] = jnp.zeros_like(chosen)
    both[...] = jnp.zeros_like(both)
    def local_pair(code):
        return lax.rem(jnp.maximum(code, 0), local)

    def place(q, code):
        e = local_pair(code)
        if q == last and SHIFT:
            return sum(jnp.where(e == c, at, 0) for at, c in enumerate(order))
        return e

    def column(p, slot, code):
        return p * local + local_pair(code)

    pieces = [(group, d) for group in range(len(GROUPS)) for d in near + (0,)]

    def send_near(count):
        for group, d in pieces[:count]:
            for k in range(GROUPS[group][1]):
                slot = GROUPS[group][0] + k
                code = listed[peer[d], 0, slot] if d else tasks_ref[0, slot]
                at = column(peer[d], slot, code)
                to = sent[group] if d else held[group]
                for row in range(own_rows):
                    to[peer[d], k, pl.ds(row, 1), :] = amp[row, pl.ds(at, 1), spans[group]]
            if d:
                near_copy(group, d).start()
        del pieces[:count]

    def send_tail():
        for f, d in enumerate(distant):
            for slot in range(slots):
                at = column(peer[d], slot, listed[peer[d], 0, slot])
                for row in range(own_rows):
                    tail_sent[f, slot, pl.ds(row, 1), :] = amp[row, pl.ds(at, 1), pl.ds(shared, tail)]
            tail_copy(f).start()


    def fetched(q):
        if q == last and SHIFT:
            def act(g, items):
                for item in items:
                    fetch_copy(q, *item).wait_recv()
                if g == layers - 1:
                    second_copy(q, g).start()
                own_copy(q, g).start()

            shifted(act)
            return

        if q == FETCHED[home[q]][0]:
            for j, f in fetches:
                fetch_copy(q, j, f).wait_recv()

        @pl.when(jnp.logical_not(inner))
        def _():
            second_copy(q).start()

        own_copy(q).start()

    def select(q):
        @pl.when(inner)
        def _():
            if q == last and SHIFT:
                for g in (1, 2):
                    @pl.when(grp == g)
                    def _():
                        for block in (3 - g, 3):
                            layer_copy(block, q, own_send, inward).wait_recv()
            else:
                for block in (outward, inward, second):
                    layer_copy(block, q, own_send, inward).wait_recv()
            if q in home:
                far[q][pl.ds(grp * per, per)] = landing[home[q]][:, :, :, landed(q)]
            for slot in range(slots):
                pick_sent[q][slot] = far[q][place(q, outer_list[0, slot])]
            pick_copy(q, outward).start()

    def near_part(group):
        for d in near:
            near_copy(group, d, True).wait_recv()
        for k in range(GROUPS[group][1]):
            slot = GROUPS[group][0] + k
            both[slot] += multiply(rows[slot, :, spans[group]], held[group][:, k])

    def far_part(q):
        @pl.when(inner)
        def _():
            for slot in range(slots):
                for f, d in enumerate(distant):
                    chosen[slot, peer[d], :, :CHUNKS[q]] = far[q][place(q, tasks_ref[0, slot]), f]

        @pl.when(jnp.logical_not(inner))
        def _():
            pick_copy(q, inward).wait_recv()
            for slot in range(slots):
                for f, d in enumerate(distant):
                    chosen[slot, peer[d], :, :CHUNKS[q]] = pick_held[q][slot, f]

        for slot in range(slots):
            both[slot] += multiply(rows[slot, :, pl.ds(starts[q], CHUNKS[q])], chosen[slot, :, :, :CHUNKS[q]])

    def tail_part():
        for f in range(len(distant)):
            tail_copy(f).wait_recv()
        for slot in range(slots):
            for f, d in enumerate(distant):
                chosen[slot, peer[d], :, :tail] = tail_held[f, slot]
            both[slot] += multiply(rows[slot, :, pl.ds(shared, tail)], chosen[slot, :, :, :tail])

    @pl.when(inner)
    def _():
        outer_copy.wait_recv()

    fetched(0)
    fetched(1)
    load_amp.wait()
    for d in range(1, n):
        list_copy(d, True).wait_recv()
    send_near(STEP)
    select(0)
    send_near(STEP)
    load_int.start()
    for q in range(2, chunks):
        send_near(2)
        fetched(q)
        if q == 2 and tail:
            send_tail()
        if q < last:
            select(q - 1)
    send_near(len(pieces))
    load_int.wait()

    @pl.loop(0, slots)
    def _(slot):
        rows[slot] = split(blocks[slot])

    for q in range(max(1, last - 1), chunks):
        select(q)
    for d in range(1, n):
        list_copy(d).wait_send()
    for q in range(chunks - SHIFT):
        if q == FETCHED[home[q]][0]:
            for j, f in fetches:
                fetch_copy(q, j, f).wait_send()
        own_copy(q).wait_send()
    if SHIFT:
        shifted(lambda g, items: [fetch_copy(last, *item).wait_send() for item in items]
                + [own_copy(last, g).wait_send()])
    for q in range(EARLY):
        far_part(q)
    near_part(0)
    for q in range(EARLY, chunks):
        far_part(q)
    if tail:
        tail_part()
    totals = functools.partial(tile_totals, tasks_ref, both, total, n, local, width, out_ref.shape[0], pack)
    last_slot = GROUPS[-1][0]
    totals(range(last_slot))
    for d in near:
        near_copy(0, d).wait_send()
    for group in range(1, len(GROUPS)):
        near_part(group)
    totals(range(last_slot, slots), True)
    for d in (6, 7, 2, 4, 3, 5, 1):
        part_copy(d).start()
    parts[me] = total[me]
    for group in range(1, len(GROUPS)):
        for d in near:
            near_copy(group, d).wait_send()
    if tail:
        for f in range(len(distant)):
            tail_copy(f).wait_send()

    @pl.when(inner)
    def _():
        for q in range(chunks):
            pick_copy(q, outward).wait_send()

    @pl.when(jnp.logical_not(inner))
    def _():
        outer_copy.wait_send()
        for q in range(chunks - SHIFT):
            second_copy(q).wait_send()

    if SHIFT:
        @pl.when(grp == layers - 1)
        def _():
            second_copy(last, layers - 1).wait_send()

    for d in (1, 2, 4, 3, 5, 6, 7):
        part_copy(d).wait_send()
    for d in (1, 2, 4, 3, 5, 6, 7):
        part_copy(d, True).wait_recv()
    write_sum(parts, out_ref, pack)


def direct_kernel(n, columns, pack, tasks_ref, amp_ref, int_ref, out_ref, listed, amp, blocks, rows, sent, held, both,
                  total, parts, local_sem, list_send, list_recv, send_sem, recv_sem, part_send, part_recv):
    me = lax.axis_index("pair")
    grp = lax.axis_index("grp")
    own_rows, pairs, depth = amp_ref.shape
    slots, width, _ = int_ref.shape
    local = pairs // n
    lists = columns < local

    load_amp = pltpu.make_async_copy(amp_ref, amp, local_sem.at[0])
    load_int = pltpu.make_async_copy(int_ref, blocks, local_sem.at[1])
    load_amp.start()
    load_int.start()

    def other(d):
        return lax.rem(me + d, n)

    def target(p):
        return (p, grp)

    barrier = pltpu.get_barrier_semaphore()

    @pl.loop(1, n)
    def _(d):
        pl.semaphore_signal(barrier, inc=1, device_id=target(other(d)), device_id_type=MESH)

    pl.semaphore_wait(barrier, n - 1)

    def list_copy(frm, to):
        return pltpu.make_async_remote_copy(
            src_ref=tasks_ref, dst_ref=listed.at[frm], send_sem=list_send.at[to], recv_sem=list_recv.at[frm],
            device_id=target(to), device_id_type=MESH)

    def column_copy(c, frm, to):
        return pltpu.make_async_remote_copy(
            src_ref=sent.at[c, to], dst_ref=held.at[c, frm], send_sem=send_sem.at[c, to],
            recv_sem=recv_sem.at[c, frm], device_id=target(to), device_id_type=MESH)

    def part_copy(frm, to):
        return pltpu.make_async_remote_copy(
            src_ref=total.at[to], dst_ref=parts.at[frm], send_sem=part_send.at[to],
            recv_sem=part_recv.at[frm], device_id=target(to), device_id_type=MESH)

    if lists:
        @pl.loop(1, n)
        def _(d):
            list_copy(me, other(d)).start()

    load_amp.wait()

    if lists:
        @pl.loop(1, n)
        def _(d):
            list_copy(other(d), other(d)).wait_recv()

    def column(p, c, codes):
        if lists:
            return p * local + lax.rem(jnp.maximum(codes(c), 0), local)
        return p * local + c

    for c in range(columns):
        @pl.loop(1, n)
        def _(d):
            p = other(d)
            at = column(p, c, lambda k: listed[p, 0, k])
            for row in range(own_rows):
                sent[c, p, pl.ds(row, 1), :] = amp[row, pl.ds(at, 1), :]

            @pl.when(d > 1)
            def _():
                column_copy(c, me, other(d - 1)).start()

        at = column(me, c, lambda k: tasks_ref[0, k])
        for row in range(own_rows):
            held[c, me, pl.ds(row, 1), :] = amp[row, pl.ds(at, 1), :]
        column_copy(c, me, other(n - 1)).start()

    load_int.wait()

    @pl.loop(0, slots)
    def _(slot):
        rows[slot] = split(blocks[slot])

    def arrive(c):
        @pl.loop(1, n)
        def _(d):
            column_copy(c, other(d), other(d)).wait_recv()

    if lists:
        for slot in range(slots):
            arrive(slot)
            both[slot] = multiply(rows[slot], held[slot])
    else:
        for c in range(columns):
            arrive(c)

        @pl.loop(0, slots)
        def _(slot):
            both[slot] = multiply(rows[slot], held[lax.rem(jnp.maximum(tasks_ref[0, slot], 0), local)])

    tile_totals(tasks_ref, both, total, n, local, width, out_ref.shape[0], pack, range(slots))

    @pl.loop(1, n)
    def _(d):
        part_copy(me, other(d)).start()

    parts[me] = total[me]

    @pl.loop(1, n)
    def _(d):
        part_copy(other(d), other(d)).wait_recv()

    write_sum(parts, out_ref, pack)

    @pl.loop(1, n)
    def _(d):
        part_copy(me, other(d)).wait_send()
        if lists:
            list_copy(me, other(d)).wait_send()
        for c in range(columns):
            column_copy(c, me, other(d)).wait_send()


def body(n, layers, amplitudes, integrals, tasks):
    own_rows, pairs, depth = amplitudes.shape
    slots, width = integrals.shape[2:4]
    local = pairs // n
    columns = min(local, slots)
    part_rows = NT * width // n
    held_rows = n * own_rows
    pack = max(1, 128 // held_rows)
    tail = depth - sum(CHUNKS)
    planes = n == 8 and layers == 4 and local == 8 and slots == 4 and depth == 4096
    dma = pltpu.SemaphoreType.DMA
    scratch = [
        pltpu.SMEM((n, 1, slots), jnp.int32),
        pltpu.VMEM(amplitudes.shape, jnp.float32),
        pltpu.VMEM((slots, width, depth), jnp.float32),
        pltpu.VMEM((slots, 2 * width, depth), jnp.bfloat16),
    ]
    results = [
        pltpu.VMEM((slots, 2 * width, 2 * held_rows), jnp.float32),
        pltpu.VMEM((n, part_rows // pack, held_rows * pack), jnp.float32),
        pltpu.VMEM((n, part_rows // pack, held_rows * pack), jnp.float32),
    ]
    if planes:
        kernel = functools.partial(plane_kernel, layers, pack)
        scratch += [pltpu.VMEM((slots, n, own_rows, max(CHUNKS + (tail,))), jnp.float32)] + results + [
            dma, dma, dma((n,)), dma((n,)), dma((len(GROUPS), n)), dma((len(GROUPS), n)), dma((2,)), dma((2,)),
            dma((len(FETCHED) + 1, 3, 2)), dma((len(FETCHED) + 1, 3, 2)), dma((len(CHUNKS),)), dma((len(CHUNKS),)),
            dma((len(CHUNKS), layers)), dma((len(CHUNKS),)), dma((len(CHUNKS),)), dma((n,)), dma((n,)),
            pltpu.SMEM((1, slots), jnp.int32), dma, dma,
        ]
        scratch += 2 * [pltpu.VMEM((n, count, own_rows, size), jnp.float32) for _, count, _, size in GROUPS]
        scratch += [pltpu.VMEM((local, 2, own_rows, chunk), jnp.float32) for chunk in CHUNKS]
        scratch += 2 * [pltpu.VMEM((slots, 2, own_rows, chunk), jnp.float32) for chunk in CHUNKS]
        if tail:
            scratch += 2 * [pltpu.VMEM((2, slots, own_rows, tail), jnp.float32)]
    else:
        kernel = functools.partial(direct_kernel, n, columns, pack)
        scratch += 2 * [pltpu.VMEM((columns, n, own_rows, depth), jnp.float32)] + results + [
            dma((2,)), dma((n,)), dma((n,)), dma((columns, n)), dma((columns, n)), dma((n,)), dma((n,)),
        ]
    if planes:
        scratch += [pltpu.VMEM((local // layers, 2, own_rows, sum(CHUNKS[q] for q in members)), jnp.float32)
                    for members in FETCHED]
    out = pl.pallas_call(
        kernel,
        out_shape=(pltpu.VMEM if planes else jax.ShapeDtypeStruct)((part_rows, held_rows), jnp.float32),
        in_specs=[
            pl.BlockSpec(memory_space=pltpu.SMEM),
            pl.BlockSpec(memory_space=pl.ANY),
            pl.BlockSpec(memory_space=pl.ANY),
        ],
        out_specs=pl.BlockSpec(memory_space=pltpu.VMEM),
        scratch_shapes=scratch,
        compiler_params=pltpu.CompilerParams(
            collective_id=0, has_side_effects=True, vmem_limit_bytes=60 * 1024 * 1024),
    )(tasks[0], amplitudes, integrals[0, 0])
    return out[None]


def solution(mesh):
    return jax.shard_map(
        functools.partial(body, mesh.shape["pair"], mesh.shape["grp"]),
        mesh=mesh,
        in_specs=(
            P("pair", None, None),
            P("grp", "pair", None, None, None),
            P("grp", "pair", None),
        ),
        out_specs=P("grp", "pair", None),
        check_vma=False,
    )
```
